32 devices in a mesh: space: 4 (over x, core), chan: 8 (over z, y).
Axes of the slice: x: 2, y: 2, z: 4, core: 2. Of those that a mesh axis runs over, the one named last changes fastest.
Arguments:
- grid_in: bfloat16 [227, 32768], P(None, ('space', 'chan')), may hold values from -6 to 6
- grid_embed_w: bfloat16 [512, 227], replicated, may hold values from -0.375 to 0.375
- g2m_w: bfloat16 [512, 512], replicated, may hold values from -0.25 to 0.25
- pair_w: bfloat16 [4, 2, 512, 512], replicated, may hold values from -0.25 to 0.25
- second_w: bfloat16 [5, 512, 512], replicated, may hold values from -0.25 to 0.25
- first_b: float32 [6, 512], replicated, may hold values from -4 to 4
- norm_gain: float32 [5, 512], replicated, may hold values from 0.5 to 1.5
- geom_w: bfloat16 [3, 512, 4], replicated, may hold values from -3 to 3
- out_w: bfloat16 [227, 512], replicated, may hold values from -0.25 to 0.25
- out_b: float32 [227], replicated, may hold values from -4 to 4
- g2m_geom: bfloat16 [4, 49152], P(None, ('space', 'chan')), may hold values from -6 to 6
- mesh_geom: bfloat16 [4, 65536], P(None, ('space', 'chan')), may hold values from -6 to 6
- m2g_geom: bfloat16 [4, 98304], P(None, ('space', 'chan')), may hold values from -6 to 6
- g2m_send: int32 [49152], P(('space', 'chan')), may hold values from 0 to 32767, as said below
- g2m_recv: int32 [49152], P(('space', 'chan')), may hold values from 0 to 16383, as said below
- mesh_recv: int32 [65536], P(('space', 'chan')), may hold values from 0 to 16383, as said below
- mesh_slot: int32 [65536], P(('space', 'chan')), may hold values from 0 to 2047
- mesh_rows: int32 [1024, 64], P(('space', 'chan')), may hold values from 0 to 511
- m2g_send: int32 [98304], P(('space', 'chan')), may hold values from 0 to 16383, as said below
Outputs:
- prediction: float32 [227, 32768], P(None, ('space', 'chan'))
- mesh_state: bfloat16 [512, 16384], P(None, ('space', 'chan'))
The draws below stay inside these ranges and needn't reach their ends.
Inputs may be any that keep to these rules, and one draw needn't show every extreme that they name: `g2m_send`: the edges of block d (1536 edges each) send from grid cells d * 1024 - 256 to (d + 1) * 1024 + 255, within the grid. `g2m_recv`: the edges of block d (1536 edges each) end at mesh nodes d * 512 to (d + 1) * 512 - 1. `mesh_recv`: the edges of block d (2048 edges each) end at mesh nodes d * 512 to (d + 1) * 512 - 1. `m2g_send`: for grid cell g in block d = g // 1024, the edges 3g to 3g + 2 send from mesh nodes d * 512 - 128 to (d + 1) * 512 + 127, within the mesh.
All inputs are finite; a program needn't handle non-finite values.
Results may differ from the reference program's by a relative error of at most 0.0095.
Values may be sent and summed in bfloat16 or wider, within the bound.
No kernel may reach another device: no remote copies, remote signals or barrier semaphores. Data moves between devices by JAX's collectives and lax.ppermute only.
A program may use at most 128 MiB of HBM per device.

```python
import jax
import jax.numpy as jnp
from jax import lax

CH = 227
LAT = 512
EF = 4
G_DEV = 1024
M_DEV = 512
LINKS_DEV = 2048
GRID = 32768
NODES = 16384
G2M_DEV = 1536
MESH_DEV = 2048
G2M_EDGES = 49152
MESH_EDGES = 65536
SLOT = 64
HG = 256
HM = 128
DEVICES = 32


def banded(key, count, per_block, block_width, reach, limit):
    index = jnp.arange(count, dtype=jnp.int32)
    owner = index // per_block
    lower = jnp.maximum(owner * block_width - reach, 0)
    upper = jnp.minimum((owner + 1) * block_width + reach, limit)
    return jax.random.randint(key, (count,), lower, upper, dtype=jnp.int32)


def draw_g2m_send(key, part):
    return banded(jax.random.fold_in(key, 11), G2M_EDGES, G2M_DEV, G_DEV, HG, GRID)


def draw_g2m_recv(key, part):
    return banded(jax.random.fold_in(key, 12), G2M_EDGES, G2M_DEV, M_DEV, 0, NODES)


def draw_mesh_recv(key, part):
    return banded(jax.random.fold_in(key, 13), MESH_EDGES, MESH_DEV, M_DEV, 0, NODES)


def draw_m2g_send(key, part):
    return banded(jax.random.fold_in(key, 14), 3 * GRID, 3 * G_DEV, M_DEV, HM, NODES)


def place_ends(entries, rng, smallest, high):
    longest = entries.shape.index(max(entries.shape))
    spots = []
    for shift in (0, 1):
        where = [jax.random.randint(jax.random.fold_in(rng, axis), (), 0, length) for axis, length in enumerate(entries.shape)]
        where[longest] = (where[longest] + shift) % entries.shape[longest]
        spots.append(tuple(where))
    return entries.at[spots[0]].set(smallest).at[spots[1]].set(high)


def levels(key, extent, cuts, low, top_value):
    def one(axis_at, shards_of):
        heights = jax.random.uniform(jax.random.fold_in(jax.random.fold_in(key, 6), axis_at), (shards_of,), jnp.float32, low / len(cuts), top_value / len(cuts))
        return jnp.repeat(jnp.exp(heights), extent[axis_at] // shards_of).reshape((-1,) + (1,) * (len(extent) - axis_at - 1))

    gain = one(*cuts[0])
    for cut in cuts[1:]:
        gain = gain * one(*cut)
    return gain


def noise(stream_key, shape, width, bound, shards=(), held_as=jnp.bfloat16):
    level = levels(stream_key, shape, shards, -0.22, 0.18) if shards else 1.0
    values = jax.random.normal(stream_key, shape, jnp.float32) * width * level
    return jnp.minimum(jnp.maximum(values, -bound), bound).astype(held_as)


def setup_inputs(seed: int = 0) -> dict:
    key_of = jax.random.split(jax.random.key(seed), 20)
    grid_in = noise(key_of[0], (CH, GRID), 1.0, 6.0, ((1, 32),))
    grid_embed_w = noise(key_of[1], (LAT, CH), CH ** -0.5, 0.375)
    g2m_w = noise(key_of[2], (LAT, LAT), LAT ** -0.5, 0.25)
    pair_w = noise(key_of[3], (4, 2, LAT, LAT), LAT ** -0.5, 0.25)
    second_w = noise(key_of[4], (5, LAT, LAT), LAT ** -0.5, 0.25)
    first_b = noise(key_of[5], (6, LAT), 1.0, 4.0, (), jnp.float32)
    norm_gain = jnp.clip(jax.random.uniform(key_of[6], (5, LAT), jnp.float32, 0.5, 1.5), 0.5, 1.5)
    geom_w = noise(key_of[7], (3, LAT, EF), EF ** -0.5, 3.0)
    out_w = noise(key_of[8], (CH, LAT), LAT ** -0.5, 0.25)
    out_b = noise(key_of[9], (CH,), 1.0, 4.0, (), jnp.float32)
    g2m_geom = noise(key_of[10], (EF, G2M_EDGES), 1.0, 6.0, ((1, 32),))
    mesh_geom = noise(key_of[11], (EF, MESH_EDGES), 1.0, 6.0, ((1, 32),))
    m2g_geom = noise(key_of[12], (EF, 3 * GRID), 1.0, 6.0, ((1, 32),))
    g2m_send = draw_g2m_send(jax.random.fold_in(key_of[19], 71), 0)
    g2m_recv = draw_g2m_recv(jax.random.fold_in(key_of[19], 71), 0)
    mesh_recv = draw_mesh_recv(jax.random.fold_in(key_of[19], 71), 0)
    mesh_slot = place_ends(jax.random.randint(key_of[16], (MESH_EDGES,), 0, LINKS_DEV), jax.random.fold_in(key_of[16], 1), 0, LINKS_DEV - 1).astype(jnp.int32)
    mesh_rows = place_ends(jax.random.randint(key_of[17], (DEVICES * DEVICES, SLOT), 0, M_DEV), jax.random.fold_in(key_of[17], 1), 0, M_DEV - 1).astype(jnp.int32)
    m2g_send = draw_m2g_send(jax.random.fold_in(key_of[19], 71), 0)
    return dict(grid_in=grid_in, grid_embed_w=grid_embed_w, g2m_w=g2m_w, pair_w=pair_w, second_w=second_w, first_b=first_b, norm_gain=norm_gain, geom_w=geom_w, out_w=out_w, out_b=out_b, g2m_geom=g2m_geom, mesh_geom=mesh_geom, m2g_geom=m2g_geom, g2m_send=g2m_send, g2m_recv=g2m_recv, mesh_recv=mesh_recv, mesh_slot=mesh_slot, mesh_rows=mesh_rows, m2g_send=m2g_send)


eps = 1e-05

def project(weight, values):
    return jnp.dot(weight, values, preferred_element_type=jnp.float32)

def layer_norm(values, gain_rows):
    row_mean = lax.optimization_barrier(jnp.mean(values, axis=0))
    row_var = lax.optimization_barrier(jnp.mean(values * values, axis=0)) - row_mean * row_mean
    return (values - row_mean[None]) * lax.rsqrt(row_var + eps)[None] * gain_rows[:, None]

def node_sums(message, receivers, count):
    return jax.ops.segment_sum(message.astype(jnp.float32).T, receivers, num_segments=count).T

def edge_block(pre_act, weight, gain_rows):
    hidden = jax.nn.silu(pre_act).astype(jnp.bfloat16)
    return layer_norm(project(weight, hidden), gain_rows).astype(jnp.bfloat16)

def reference(grid_in, grid_embed_w, g2m_w, pair_w, second_w, first_b, norm_gain, geom_w, out_w, out_b, g2m_geom, mesh_geom, m2g_geom, g2m_send, g2m_recv, mesh_recv, mesh_slot, mesh_rows, m2g_send):
    grid_latent = edge_block(project(grid_embed_w, grid_in) + first_b[0][:, None], second_w[0], norm_gain[0])
    encode_send = project(g2m_w, grid_latent).astype(jnp.bfloat16)
    pre_act = encode_send[:, g2m_send].astype(jnp.float32) + project(geom_w[0], g2m_geom) + first_b[1][:, None]
    message = edge_block(pre_act, second_w[1], norm_gain[1])
    mesh_latent = node_sums(message, g2m_recv, NODES).astype(jnp.bfloat16)
    link_send = project(pair_w[0, 0], mesh_latent).astype(jnp.bfloat16)
    link_recv = project(pair_w[0, 1], mesh_latent)
    edge_index = jnp.arange(MESH_EDGES, dtype=jnp.int32)
    owner = (edge_index // MESH_DEV).astype(jnp.int32)
    source = (mesh_slot // SLOT).astype(jnp.int32)
    position = (mesh_slot % SLOT).astype(jnp.int32)
    senders = source * M_DEV + mesh_rows[source * DEVICES + owner, position]
    pre_act = link_send[:, senders].astype(jnp.float32) + link_recv[:, mesh_recv] + project(geom_w[1], mesh_geom) + first_b[2][:, None]
    message = edge_block(pre_act, second_w[2], norm_gain[2])
    aggregate = node_sums(message, mesh_recv, NODES).astype(jnp.bfloat16)
    node_pre = project(pair_w[1, 0], mesh_latent) + project(pair_w[1, 1], aggregate) + first_b[3][:, None]
    node_hidden = jax.nn.silu(node_pre).astype(jnp.bfloat16)
    mesh_state = (mesh_latent.astype(jnp.float32) + layer_norm(project(second_w[3], node_hidden), norm_gain[3])).astype(jnp.bfloat16)
    decode_send = project(pair_w[2, 0], mesh_state).astype(jnp.bfloat16)
    decode_grid = project(pair_w[2, 1], grid_latent)
    expanded = jnp.broadcast_to(decode_grid[:, :, None], (LAT, GRID, 3)).reshape(LAT, 3 * GRID)
    pre_act = decode_send[:, m2g_send].astype(jnp.float32) + expanded + project(geom_w[2], m2g_geom) + first_b[4][:, None]
    message = edge_block(pre_act, second_w[4], norm_gain[4])
    gathered = message.astype(jnp.float32).reshape(LAT, GRID, 3).sum(axis=2).astype(jnp.bfloat16)
    out_pre = project(pair_w[3, 0], grid_latent) + project(pair_w[3, 1], gathered) + first_b[5][:, None]
    out_hidden = jax.nn.silu(out_pre).astype(jnp.bfloat16)
    prediction = project(out_w, out_hidden) + out_b[:, None]
    return (prediction, mesh_state)
```

```python
import functools

import jax
import jax.numpy as jnp
from jax import lax
from jax.experimental import pallas as pl
from jax.experimental.pallas import tpu as pltpu
from jax.sharding import PartitionSpec as P

M_DEV = 512
BLOCK = 256

eps = 1e-05
bf16 = jnp.bfloat16
f32 = jnp.float32


def contract(left, right, left_dim, right_dim):
    return lax.dot_general(
        left, right, (((left_dim,), (right_dim,)), ((), ())), preferred_element_type=f32
    )


def nn(left, right):
    return contract(left, right, 1, 0)


def nt(left, right):
    return contract(left, right, 1, 1)


def tn(left, right):
    return contract(left, right, 0, 0)


def swish(values):
    half = values * 0.5
    return half * jnp.tanh(half) + half


def norm_columns(values, gain):
    count = 1.0 / values.shape[0]
    mean = jnp.sum(values, axis=0, keepdims=True) * count
    var = jnp.sum(values * values, axis=0, keepdims=True) * count - mean * mean
    return (values - mean) * lax.rsqrt(var + eps) * gain


def pick_rows(index_row, count):
    rows = lax.broadcasted_iota(jnp.int32, (count, index_row.shape[1]), 0)
    return jnp.where(rows == index_row, 1.0, 0.0).astype(bf16)


def pick_columns(index_column, count):
    columns = lax.broadcasted_iota(jnp.int32, (index_column.shape[0], count), 1)
    return jnp.where(columns == index_column, 1.0, 0.0).astype(bf16)


def blocks(total):
    return [pl.ds(start, BLOCK) for start in range(0, total, BLOCK)]


def embed_columns(x, embed_w, second_w, bias, gain):
    hidden = swish(nn(embed_w, x) + bias).astype(bf16)
    return norm_columns(nn(second_w, hidden), gain).astype(bf16)


def embed_kernel(x, embed_w, second_w, send_w, bias, gain, latent, send):
    for part in blocks(x.shape[1]):
        cells = embed_columns(x[:, part], embed_w[...], second_w[...], bias[...], gain[...])
        latent[:, part] = cells
        send[:, part] = nn(send_w[...], cells).astype(bf16)


def encode_kernel(
    own,
    low,
    high,
    embed_w,
    embed_second_w,
    send_w,
    embed_bias,
    embed_gain,
    geom,
    geom_w,
    send_index,
    recv_index,
    edge_w,
    edge_gain,
    link_w,
    slot_rows,
    latent,
    outgoing,
    table,
    picks,
    messages,
    sums,
):
    reach = low.shape[1]
    cells = own.shape[1]
    edges = geom.shape[1]
    ext = cells + 2 * reach
    width = own.shape[0]
    table[:, reach : reach + cells] = own[...]
    for start, halo in ((0, low), (reach + cells, high)):
        values = embed_columns(
            halo[...], embed_w[...], embed_second_w[...], embed_bias[...], embed_gain[...]
        )
        table[:, start : start + reach] = nn(send_w[...], values).astype(bf16)
    table[:, ext:] = geom_w[...]
    for part in blocks(edges):
        picks[:ext, :] = pick_rows(send_index[:, part], ext)
        picks[ext:, :] = geom[:, part]
        hidden = swish(nn(table[...], picks[...])).astype(bf16)
        messages[:, part] = norm_columns(nn(edge_w[...], hidden), edge_gain[...]).astype(bf16)
        sums[:, part] = pick_rows(recv_index[:, part], sums.shape[0])
    nodes = nt(sums[...], messages[...]).astype(bf16)
    latent[...] = nodes
    link = nt(nodes, link_w[...]).astype(bf16)
    for part in blocks(outgoing.shape[0]):
        outgoing[part, :] = nn(pick_columns(slot_rows[part, :], width), link).astype(bf16)


def window_kernel(
    latent,
    recv_column,
    recv_w,
    mesh_geom,
    mesh_geom_w,
    node_w,
    node_bias,
    grid_latent,
    decode_w,
    out_w,
    out_bias,
    cell_geom,
    cell_geom_w,
    recv_terms,
    node_terms,
    latent_columns,
    cell_terms,
    out_terms,
):
    nodes = latent[...]
    for part in blocks(recv_terms.shape[0]):
        picked = nn(pick_columns(recv_column[part, :], nodes.shape[0]), nodes).astype(bf16)
        recv_terms[part, :] = nt(picked, recv_w[...]) + tn(mesh_geom[:, part], mesh_geom_w[...])
    node_terms[...] = nt(node_w[...], nodes) + node_bias[...]
    latent_columns[...] = jnp.transpose(nodes.astype(f32))
    for part in blocks(grid_latent.shape[1]):
        cells = grid_latent[:, part]
        out_terms[:, part] = nn(out_w[...], cells) + out_bias[...]
        terms = nn(decode_w[...], cells)
        for k in range(cell_terms.shape[0]):
            cell_terms[k, :, part] = terms + nn(cell_geom_w[...], cell_geom[k, :, part])


def mesh_kernel(
    arrived,
    slot_column,
    recv_terms,
    recv_index,
    edge_w,
    edge_gain,
    node_terms,
    node_w,
    node_second_w,
    node_gain,
    latent_columns,
    send_w,
    state,
    send,
    send_low,
    send_high,
    messages,
    sums,
):
    reach = send_low.shape[1]
    for part in blocks(recv_terms.shape[0]):
        picks = pick_columns(slot_column[part, :], arrived.shape[0])
        hidden = swish(nn(picks, arrived[...]) + recv_terms[part, :]).astype(bf16)
        messages[:, part] = norm_columns(nt(edge_w[...], hidden), edge_gain[...]).astype(bf16)
        sums[:, part] = pick_rows(recv_index[:, part], sums.shape[0])
    nodes = nt(sums[...], messages[...]).astype(bf16)
    hidden = swish(nt(node_w[...], nodes) + node_terms[...]).astype(bf16)
    values = latent_columns[...] + norm_columns(nn(node_second_w[...], hidden), node_gain[...])
    values = values.astype(bf16)
    state[...] = values
    sent = nn(send_w[...], values).astype(bf16)
    send[...] = sent
    send_low[...] = sent[:, :reach]
    send_high[...] = sent[:, sent.shape[1] - reach :]


def local_kernel(send, index, terms, out):
    for k in range(terms.shape[0]):
        out[k] = terms[k] + nn(send[...], pick_rows(index[k], send.shape[1]))


def decode_kernel(
    low, high, index, terms, edge_w, edge_gain, out_terms, gathered_w, out_w, out_bias, prediction
):
    reach = low.shape[1]
    halo = jnp.concatenate([low[...], high[...]], axis=1)
    total = None
    for k in range(terms.shape[0]):
        hidden = swish(terms[k] + nn(halo, pick_rows(index[k], 2 * reach))).astype(bf16)
        message = norm_columns(nn(edge_w[...], hidden), edge_gain[...]).astype(bf16).astype(f32)
        total = message if total is None else total + message
    hidden = swish(out_terms[...] + nn(gathered_w[...], total.astype(bf16))).astype(bf16)
    prediction[...] = nn(out_w[...], hidden) + out_bias[...]


def call(kernel, outs, *args, scratch=()):
    return pl.pallas_call(
        kernel,
        out_shape=outs,
        scratch_shapes=scratch,
        compiler_params=pltpu.CompilerParams(vmem_limit_bytes=56 << 20),
    )(*args)


def split_bias(bias):
    high = bias.astype(bf16)
    rest = bias - high.astype(f32)
    middle = rest.astype(bf16)
    low = (rest - middle.astype(f32)).astype(bf16)
    return jnp.stack([high, middle, low], axis=-1)


def exchange(low_end, high_end):
    axes = ("space", "chan")
    count = lax.axis_size("space") * lax.axis_size("chan")
    up = [(i, (i + 1) % count) for i in range(count)]
    down = [(target, source) for source, target in up]
    return lax.ppermute(high_end, axes, up), lax.ppermute(low_end, axes, down)


def body(
    grid_in,
    grid_embed_w,
    g2m_w,
    pair_w,
    second_w,
    first_b,
    norm_gain,
    geom_w,
    out_w,
    out_b,
    g2m_geom,
    mesh_geom,
    m2g_geom,
    g2m_send,
    g2m_recv,
    mesh_recv,
    mesh_slot,
    mesh_rows,
    m2g_send,
):
    width = grid_embed_w.shape[0]
    cells = grid_in.shape[1]
    position = lax.axis_index(("space", "chan"))
    reach = cells // 4
    low, high = exchange(grid_in[:, :reach], grid_in[:, cells - reach :])

    bias_columns = first_b.T
    gain_columns = norm_gain.T
    bias = lambda i: bias_columns[:, i : i + 1]
    gain = lambda i: gain_columns[:, i : i + 1]
    shape = jax.ShapeDtypeStruct

    def geom_weights(i, bias_index, pad):
        weights = jnp.concatenate([geom_w[i], split_bias(first_b[bias_index])], axis=1)
        return jnp.pad(weights, ((0, 0), (0, pad - weights.shape[1])))

    def geom_rows(values, pad):
        lead = values.shape[:-2]
        edges = values.shape[-1]
        used = values.shape[-2] + 3
        return jnp.concatenate(
            [values, jnp.ones(lead + (3, edges), bf16), jnp.zeros(lead + (pad - used, edges), bf16)],
            axis=-2,
        )

    grid_latent, own_send = call(
        embed_kernel,
        (shape((width, cells), bf16), shape((width, cells), bf16)),
        grid_in,
        grid_embed_w,
        second_w[0],
        g2m_w,
        bias(0),
        gain(0),
    )

    edges = g2m_geom.shape[1]
    pad = 128
    ext = cells + 2 * reach
    slots = mesh_rows.size
    latent, outgoing = call(
        encode_kernel,
        (shape((M_DEV, width), bf16), shape((slots, width), bf16)),
        own_send,
        low,
        high,
        grid_embed_w,
        second_w[0],
        g2m_w,
        bias(0),
        gain(0),
        geom_rows(g2m_geom, pad),
        geom_weights(0, 1, pad),
        (g2m_send - position * cells + reach)[None, :],
        (g2m_recv - position * M_DEV)[None, :],
        second_w[1],
        gain(1),
        pair_w[0, 0],
        mesh_rows.reshape(-1, 1),
        scratch=[
            pltpu.VMEM((width, ext + pad), bf16),
            pltpu.VMEM((ext + pad, BLOCK), bf16),
            pltpu.VMEM((width, edges), bf16),
            pltpu.VMEM((M_DEV, edges), bf16),
        ],
    )
    arrived = lax.all_to_all(
        outgoing.reshape(mesh_rows.shape + (width,)),
        ("space", "chan"),
        split_axis=0,
        concat_axis=0,
        tiled=True,
    ).reshape(-1, width)

    mesh_edges = mesh_geom.shape[1]
    recv_local = mesh_recv - position * M_DEV
    per_cell = m2g_send.shape[0] // cells
    cell_geom = m2g_geom.reshape(-1, cells, per_cell).transpose(2, 0, 1)
    recv_terms, node_terms, latent_columns, cell_terms, out_terms = call(
        window_kernel,
        (
            shape((mesh_edges, width), f32),
            shape((width, M_DEV), f32),
            shape((width, M_DEV), f32),
            shape((per_cell, width, cells), f32),
            shape((width, cells), f32),
        ),
        latent,
        recv_local.reshape(-1, 1),
        pair_w[0, 1],
        geom_rows(mesh_geom, 8),
        geom_weights(1, 2, 8).T,
        pair_w[1, 0],
        bias(3),
        grid_latent,
        pair_w[2, 1],
        pair_w[3, 0],
        bias(5),
        geom_rows(cell_geom, 8),
        geom_weights(2, 4, 8),
    )

    mesh_reach = M_DEV // 4
    state, send, send_low, send_high = call(
        mesh_kernel,
        (
            shape((width, M_DEV), bf16),
            shape((width, M_DEV), bf16),
            shape((width, mesh_reach), bf16),
            shape((width, mesh_reach), bf16),
        ),
        arrived,
        mesh_slot.reshape(-1, 1),
        recv_terms,
        recv_local[None, :],
        second_w[2],
        gain(2),
        node_terms,
        pair_w[1, 1],
        second_w[3],
        gain(3),
        latent_columns,
        pair_w[2, 0],
        scratch=[
            pltpu.VMEM((width, mesh_edges), bf16),
            pltpu.VMEM((M_DEV, mesh_edges), bf16),
        ],
    )
    low, high = exchange(send_low, send_high)

    own_index = (m2g_send - position * M_DEV).reshape(cells, per_cell).T[:, None, :]
    halo_index = jnp.where(
        own_index < 0,
        own_index + mesh_reach,
        jnp.where(own_index >= M_DEV, own_index - M_DEV + mesh_reach, -1),
    )
    whole = lambda *dims: pl.BlockSpec(dims, lambda i: (0,) * len(dims))
    index_spec = pl.BlockSpec((per_cell, 1, BLOCK), lambda i: (0, 0, i))
    terms_spec = pl.BlockSpec((per_cell, width, BLOCK), lambda i: (0, 0, i))
    params = pltpu.CompilerParams(vmem_limit_bytes=56 << 20)
    cell_terms = pl.pallas_call(
        local_kernel,
        grid=(cells // BLOCK,),
        in_specs=[whole(width, M_DEV), index_spec, terms_spec],
        out_specs=terms_spec,
        out_shape=shape(cell_terms.shape, f32),
        compiler_params=params,
    )(send, own_index, cell_terms)
    channels = out_w.shape[0]
    prediction = pl.pallas_call(
        decode_kernel,
        grid=(cells // BLOCK,),
        in_specs=[
            whole(width, mesh_reach),
            whole(width, mesh_reach),
            index_spec,
            terms_spec,
            whole(width, width),
            whole(width, 1),
            pl.BlockSpec((width, BLOCK), lambda i: (0, i)),
            whole(width, width),
            whole(channels, width),
            whole(channels, 1),
        ],
        out_specs=pl.BlockSpec((channels, BLOCK), lambda i: (0, i)),
        out_shape=shape((channels, cells), f32),
        compiler_params=params,
    )(
        low,
        high,
        halo_index,
        cell_terms,
        second_w[4],
        gain(4),
        out_terms,
        pair_w[3, 1],
        out_w,
        out_b[:, None],
    )
    return (prediction, state)


def solution(mesh):
    split = ("space", "chan")
    return jax.shard_map(
        body,
        mesh=mesh,
        in_specs=(
            P(None, split),
            P(),
            P(),
            P(),
            P(),
            P(),
            P(),
            P(),
            P(),
            P(),
            P(None, split),
            P(None, split),
            P(None, split),
            P(split),
            P(split),
            P(split),
            P(split),
            P(split, None),
            P(split),
        ),
        out_specs=(P(None, split), P(None, split)),
        check_vma=False,
    )
```

```python
import jax
import jax.numpy as jnp
from jax import lax
from jax.experimental import pallas as pl
from jax.experimental.pallas import tpu as pltpu
from jax.sharding import PartitionSpec as P

M_DEV = 512
BLOCK = 512
VMEM_LIMIT = 16 << 20

eps = 1e-05
bf16 = jnp.bfloat16
f32 = jnp.float32


def contract(left, right, left_dim, right_dim):
    return lax.dot_general(
        left, right, (((left_dim,), (right_dim,)), ((), ())), preferred_element_type=f32
    )


def nn(left, right):
    return contract(left, right, 1, 0)


def nt(left, right):
    return contract(left, right, 1, 1)


def tn(left, right):
    return contract(left, right, 0, 0)


def swish(values):
    half = values * 0.5
    return half * jnp.tanh(half) + half


def norm_columns(values, gain):
    count = 1.0 / values.shape[0]
    mean = jnp.sum(values, axis=0, keepdims=True) * count
    var = jnp.sum(values * values, axis=0, keepdims=True) * count - mean * mean
    return (values - mean) * lax.rsqrt(var + eps) * gain


def pick_rows(index_row, count):
    rows = lax.broadcasted_iota(jnp.int16, (count, index_row.shape[1]), 0)
    return jnp.where(rows == index_row.astype(jnp.int16), bf16(1), bf16(0))


def pick_columns(index_column, count):
    columns = lax.broadcasted_iota(jnp.int16, (index_column.shape[0], count), 1)
    return jnp.where(columns == index_column.astype(jnp.int16), bf16(1), bf16(0))


def blocks(total):
    return [pl.ds(start, BLOCK) for start in range(0, total, BLOCK)]


def embed_columns(x, embed_w, second_w, bias, gain):
    hidden = swish(tn(embed_w, x) + bias).astype(bf16)
    return norm_columns(nn(second_w, hidden), gain).astype(bf16)


class Fetch:
    def __init__(self, source, buffer, semaphore):
        self.copy = pltpu.make_async_copy(source, buffer, semaphore)
        self.copy.start()
        self.buffer = buffer
        self.arrived = False

    def __call__(self):
        if not self.arrived:
            self.copy.wait()
            self.arrived = True
        return self.buffer


def column(rows, i):
    return jnp.transpose(rows[...])[:, i : i + 1]


def index_row(index, part):
    return index[part].reshape(1, -1)


def index_column(index, part):
    row = index_row(index, part).astype(f32)
    return jnp.transpose(jnp.broadcast_to(row, (8, row.shape[1])))[:, :1].astype(jnp.int32)


def embed_kernel(x, embed_w, biases, second_w, gains, send_w, latent, send):
    bias = column(biases(), 0)
    for part in blocks(x().shape[1]):
        hidden = swish(tn(embed_w()[...], x()[:, part]) + bias).astype(bf16)
        cells = norm_columns(nn(second_w()[...], hidden), column(gains(), 0)).astype(bf16)
        latent[:, part] = cells
        send[:, part] = nn(send_w()[...], cells).astype(bf16)


def encode_kernel(
    grid_latent,
    own,
    low,
    high,
    embed_w,
    embed_second_w,
    send_w,
    biases,
    gains,
    geom,
    geom_w,
    send_index,
    recv_index,
    edge_w,
    rows,
    link_w,
    grid_latent_out,
    latent,
    outgoing,
    table,
    messages,
    sums,
    picks,
    staged,
    nodes_near,
    semaphores,
):
    copies = [pltpu.make_async_copy(grid_latent, grid_latent_out, semaphores.at[0])]
    copies[0].start()
    halo = jnp.concatenate([low[...], high[...]], axis=1)
    reach = halo.shape[1] // 2
    cells = own.shape[1]
    ext = cells + 2 * reach
    table[:, reach : reach + cells] = own[...]
    halo = embed_columns(
        halo, embed_w[...], embed_second_w[...], column(biases, 0), column(gains, 0)
    )
    halo = nn(send_w[...], halo).astype(bf16)
    table[:, :reach] = halo[:, :reach]
    table[:, reach + cells :] = halo[:, reach:]
    bias = column(biases, 1)
    gain = column(gains, 1)
    for part in blocks(geom.shape[1]):
        pre_act = nn(table[...], pick_rows(index_row(send_index, part), ext))
        pre_act = pre_act + tn(geom_w[...], geom[:, part]) + bias
        hidden = swish(pre_act).astype(bf16)
        messages[:, part] = norm_columns(nn(edge_w[...], hidden), gain).astype(bf16)
        sums[:, part] = pick_rows(index_row(recv_index, part), sums.shape[0])
    row_columns = jnp.transpose(rows[...].astype(f32))
    per_row, count = row_columns.shape
    lanes = lax.broadcasted_iota(jnp.int32, (per_row, latent.shape[0]), 1).astype(f32)
    for i in range(count):
        picked = jnp.where(lanes == row_columns[:, i : i + 1], 1.0, 0.0)
        picks[i * per_row : (i + 1) * per_row, :] = picked.astype(bf16)
    nodes = nt(sums[...], messages[...]).astype(bf16)
    nodes_near[...] = nodes
    copies.append(pltpu.make_async_copy(nodes_near, latent, semaphores.at[1]))
    copies[-1].start()
    link = nt(nodes, link_w[...]).astype(bf16)
    for part in blocks(outgoing.shape[0]):
        staged[part, :] = nn(picks[part, :], link).astype(bf16)
        copies.append(
            pltpu.make_async_copy(
                staged.at[part, :], outgoing.at[part, :], semaphores.at[len(copies)]
            )
        )
        copies[-1].start()
    for copy in copies:
        copy.wait()


def window_kernel(
    latent,
    mesh_geom,
    recv_w,
    biases,
    mesh_geom_w,
    recv_index,
    node_w,
    grid_latent,
    decode_w,
    out_w,
    cell_geom_w,
    cell_geom,
    recv_terms,
    node_terms,
    latent_columns,
    cell_terms,
    out_terms,
):
    nodes = latent()[...]
    recv_bias = biases()[2:3, :]
    for part in blocks(recv_terms.shape[0]):
        picked = pick_columns(index_column(recv_index(), part), nodes.shape[0])
        picked = nn(picked, nodes).astype(bf16)
        terms = nt(picked, recv_w()[...]) + tn(mesh_geom()[:, part], mesh_geom_w()[...])
        recv_terms[part, :] = terms + recv_bias
    node_terms[...] = nt(node_w()[...], nodes) + column(biases(), 3)
    latent_columns[...] = jnp.transpose(nodes.astype(f32)).astype(bf16)
    cell_bias = column(biases(), 4)
    out_bias = column(biases(), 5)
    for part in blocks(grid_latent().shape[1]):
        cells = grid_latent()[:, part]
        out_terms[:, part] = nn(out_w()[...], cells) + out_bias
        terms = nn(decode_w()[...], cells) + cell_bias
        for k in range(cell_terms.shape[0]):
            cell_terms[k, :, part] = terms + tn(cell_geom_w()[...], cell_geom()[k, :, part])


def mesh_kernel(slot_index, edge_w, gains, recv_index, *refs):
    *recv_terms, node_w, node_terms, node_second_w, latent_columns, send_w = refs[:-8]
    arrived, state, send, send_low, send_high, messages, staged, semaphore = refs[-8:]
    reach = send_low.shape[1]
    sums = []
    for part, terms in zip(blocks(messages.shape[1]), recv_terms):
        picks = pick_columns(index_column(slot_index(), part), arrived.shape[0])
        hidden = swish(nn(picks, arrived[...]) + terms()[...]).astype(bf16)
        normed = norm_columns(nt(edge_w()[...], hidden), column(gains(), 2))
        messages[:, part] = normed.astype(bf16)
        sums.append(pick_rows(index_row(recv_index(), part), state.shape[1]))
    nodes = nt(jnp.concatenate(sums, axis=1), messages[...]).astype(bf16)
    hidden = swish(nt(node_w()[...], nodes) + node_terms()[...]).astype(bf16)
    normed = norm_columns(nn(node_second_w()[...], hidden), column(gains(), 3))
    values = (latent_columns()[...].astype(f32) + normed).astype(bf16)
    staged[...] = values
    copy = pltpu.make_async_copy(staged, state, semaphore)
    copy.start()
    sent = nn(send_w()[...], values).astype(bf16)
    send[...] = sent
    send_low[...] = sent[:, :reach]
    send_high[...] = sent[:, sent.shape[1] - reach :]
    copy.wait()


def local_kernel(index, *refs):
    *terms, send, out = refs
    for k in range(out.shape[0]):
        for part in blocks(out.shape[2]):
            picks = pick_rows(index()[k, :, part], send.shape[1])
            out[k, :, part] = terms[k]()[:, part] + nn(send[...], picks)


def decode_kernel(
    low,
    high,
    index,
    terms,
    edge_w,
    gains,
    gathered_w,
    out_terms,
    out_w,
    out_bias,
    prediction,
    staged,
    semaphores,
):
    halo = jnp.concatenate([low[...], high[...]], axis=1)
    gain = column(gains, 4)
    copies = []
    for part in blocks(terms.shape[2]):
        total = None
        for k in range(terms.shape[0]):
            picks = pick_rows(index[k, :, part], halo.shape[1])
            hidden = swish(terms[k, :, part] + nn(halo, picks)).astype(bf16)
            message = norm_columns(nn(edge_w[...], hidden), gain).astype(bf16).astype(f32)
            total = message if total is None else total + message
        pre_act = out_terms[:, part] + nn(gathered_w[...], total.astype(bf16))
        hidden = swish(pre_act).astype(bf16)
        staged[:, part] = nn(out_w[...], hidden) + out_bias[...]
        copies.append(
            pltpu.make_async_copy(
                staged.at[:, part], prediction.at[:, part], semaphores.at[len(copies)]
            )
        )
        copies[-1].start()
    for copy in copies:
        copy.wait()


def part_shape(shape, index):
    lead = tuple(part.size for part in index if isinstance(part, pl.Slice))
    return lead + shape[len(index) :]


def fetching(
    kernel,
    outs,
    fetched=(),
    resident=(),
    carried=(),
    scratch=(),
    in_place=(),
    limit=VMEM_LIMIT,
):
    pairs = [item if isinstance(item, tuple) else (item, ()) for item in fetched]
    n_in, n_res, n_out = len(pairs), len(resident), len(outs)
    extra = []
    for item in carried:
        if isinstance(item, int):
            extra.append(item)
        else:
            pairs.append(item if isinstance(item, tuple) else (item, ()))
            extra.append(len(pairs) - 1)
    arrays = [array for array, _ in pairs]
    shapes = [(part_shape(array.shape, index), array.dtype) for array, index in pairs]
    local = [i for i in range(len(pairs)) if i not in extra]

    def run(*refs):
        sources, refs = refs[: len(pairs)], refs[len(pairs) :]
        near, refs = refs[:n_res], refs[n_res:]
        results, refs = refs[:n_out], refs[n_out:]
        passed, refs = refs[: len(extra)], refs[len(extra) :]
        buffers = dict(zip(extra, passed))
        buffers.update(zip(local, refs[: len(local)]))
        refs = refs[len(local) :]
        copies = []
        if pairs:
            for i, (source, (_, index)) in enumerate(zip(sources, pairs)):
                source = source.at[index] if index else source
                copies.append(Fetch(source, buffers[i], refs[0].at[i]))
            refs = refs[1:]
        kernel(*copies[:n_in], *near, *results, *refs)
        for copy in copies:
            copy()

    near = pl.BlockSpec(memory_space=pltpu.VMEM)
    far = pl.BlockSpec(memory_space=pltpu.HBM)
    return pl.pallas_call(
        run,
        out_shape=tuple(outs) + tuple(pltpu.VMEM(*shapes[i]) for i in extra),
        in_specs=[far] * len(pairs) + [near] * n_res,
        out_specs=tuple(far if i in in_place else near for i in range(n_out))
        + (near,) * len(extra),
        scratch_shapes=[pltpu.VMEM(*shapes[i]) for i in local]
        + ([pltpu.SemaphoreType.DMA((len(pairs),))] if pairs else [])
        + list(scratch),
        compiler_params=pltpu.CompilerParams(vmem_limit_bytes=limit),
    )(
        *[pltpu.with_memory_space_constraint(value, pltpu.HBM) for value in arrays],
        *[pltpu.with_memory_space_constraint(value, pltpu.VMEM) for value in resident],
    )


def exchange(low_end, high_end):
    axes = ("space", "chan")
    count = lax.axis_size("space") * lax.axis_size("chan")
    up = [(i, (i + 1) % count) for i in range(count)]
    down = [(target, source) for source, target in up]
    return lax.ppermute(high_end, axes, up), lax.ppermute(low_end, axes, down)


def body(
    grid_in,
    grid_embed_w,
    g2m_w,
    pair_w,
    second_w,
    first_b,
    norm_gain,
    geom_w,
    out_w,
    out_b,
    g2m_geom,
    mesh_geom,
    m2g_geom,
    g2m_send,
    g2m_recv,
    mesh_recv,
    mesh_slot,
    mesh_rows,
    m2g_send,
):
    width = grid_embed_w.shape[0]
    cells = grid_in.shape[1]
    position = lax.axis_index(("space", "chan"))
    reach = cells // 4
    low, high = exchange(grid_in[:, :reach], grid_in[:, cells - reach :])

    kept = pltpu.VMEM
    shape = pltpu.HBM
    embed_t = grid_embed_w.T
    geom_t = geom_w.transpose(0, 2, 1)
    (
        grid_latent,
        own_send,
        embed_near,
        embed_second_near,
        g2m_near,
        bias_near,
        gain_near,
        geom_near,
        geom_w_near,
        send_near,
        recv_near,
        edge_near,
        rows_near,
        link_near,
    ) = fetching(
        embed_kernel,
        (kept((width, cells), bf16), kept((width, cells), bf16)),
        [grid_in, embed_t, first_b, (second_w, (0,)), norm_gain, g2m_w],
        carried=[
            1,
            3,
            5,
            2,
            4,
            g2m_geom,
            (geom_t, (0,)),
            g2m_send - position * cells + reach,
            g2m_recv - position * M_DEV,
            (second_w, (1,)),
            mesh_rows,
            (pair_w, (0, 0)),
        ],
    )

    edges = g2m_geom.shape[1]
    slots = mesh_rows.size
    grid_latent, latent, outgoing = fetching(
        encode_kernel,
        (
            shape((width, cells), bf16),
            shape((M_DEV, width), bf16),
            shape((slots, width), bf16),
        ),
        resident=[
            grid_latent,
            own_send,
            low,
            high,
            embed_near,
            embed_second_near,
            g2m_near,
            bias_near,
            gain_near,
            geom_near,
            geom_w_near,
            send_near,
            recv_near,
            edge_near,
            rows_near,
            link_near,
        ],
        scratch=[
            pltpu.VMEM((width, cells + 2 * reach), bf16),
            pltpu.VMEM((width, edges), bf16),
            pltpu.VMEM((M_DEV, edges), bf16),
            pltpu.VMEM((slots, M_DEV), bf16),
            pltpu.VMEM((slots, width), bf16),
            pltpu.VMEM((M_DEV, width), bf16),
            pltpu.SemaphoreType.DMA((2 + slots // BLOCK,)),
        ],
        in_place=(0, 1, 2),
    )
    arrived = lax.all_to_all(
        outgoing.reshape(mesh_rows.shape + (width,)),
        ("space", "chan"),
        split_axis=0,
        concat_axis=0,
        tiled=True,
    ).reshape(-1, width)

    mesh_edges = mesh_geom.shape[1]
    mesh_reach = M_DEV // 4
    recv_local = mesh_recv - position * M_DEV
    per_cell = m2g_send.shape[0] // cells
    cell_geom = m2g_geom.reshape(-1, cells, per_cell).transpose(2, 0, 1)
    own_index = (m2g_send - position * M_DEV).reshape(cells, per_cell).T[:, None, :]
    halo_index = jnp.where(
        own_index < 0,
        own_index + mesh_reach,
        jnp.where(own_index >= M_DEV, own_index - M_DEV + mesh_reach, -1),
    )
    recv_terms, node_terms, latent_columns, cell_terms, out_terms = fetching(
        window_kernel,
        (
            shape((mesh_edges, width), f32),
            shape((width, M_DEV), f32),
            shape((width, M_DEV), bf16),
            shape((per_cell, width, cells), f32),
            shape((width, cells), f32),
        ),
        [
            latent,
            mesh_geom,
            (pair_w, (0, 1)),
            first_b,
            (geom_t, (1,)),
            recv_local,
            (pair_w, (1, 0)),
            grid_latent,
            (pair_w, (2, 1)),
            (pair_w, (3, 0)),
            (geom_t, (2,)),
            cell_geom,
        ],
        limit=40 << 20,
    )

    state, send, send_low, send_high = fetching(
        mesh_kernel,
        (
            shape((width, M_DEV), bf16),
            kept((width, M_DEV), bf16),
            kept((width, mesh_reach), bf16),
            kept((width, mesh_reach), bf16),
        ),
        [mesh_slot, (second_w, (2,)), norm_gain, recv_local]
        + [(recv_terms, (part,)) for part in blocks(mesh_edges)]
        + [
            (pair_w, (1, 1)),
            node_terms,
            (second_w, (3,)),
            latent_columns,
            (pair_w, (2, 0)),
        ],
        resident=[arrived],
        scratch=[
            pltpu.VMEM((width, mesh_edges), bf16),
            pltpu.VMEM((width, M_DEV), bf16),
            pltpu.SemaphoreType.DMA(()),
        ],
        in_place=(0,),
        limit=32 << 20,
    )
    low, high = exchange(send_low, send_high)
    (
        cell_terms,
        halo_near,
        decode_near,
        gain_near,
        gathered_near,
        out_terms,
        out_w_near,
        out_b_near,
    ) = fetching(
        local_kernel,
        (kept(cell_terms.shape, f32),),
        [own_index] + [(cell_terms, (k,)) for k in range(per_cell)],
        resident=[send],
        carried=[
            halo_index,
            (second_w, (4,)),
            norm_gain,
            (pair_w, (3, 1)),
            out_terms,
            out_w,
            out_b[:, None],
        ],
    )
    (prediction,) = fetching(
        decode_kernel,
        (shape((out_w.shape[0], cells), f32),),
        resident=[
            low,
            high,
            halo_near,
            cell_terms,
            decode_near,
            gain_near,
            gathered_near,
            out_terms,
            out_w_near,
            out_b_near,
        ],
        scratch=[
            pltpu.VMEM((out_w.shape[0], cells), f32),
            pltpu.SemaphoreType.DMA((cells // BLOCK,)),
        ],
        in_place=(0,),
    )
    return (prediction, state)


def solution(mesh):
    split = ("space", "chan")
    return jax.shard_map(
        body,
        mesh=mesh,
        in_specs=(
            P(None, split),
            P(),
            P(),
            P(),
            P(),
            P(),
            P(),
            P(),
            P(),
            P(),
            P(None, split),
            P(None, split),
            P(None, split),
            P(split),
            P(split),
            P(split),
            P(split),
            P(split, None),
            P(split),
        ),
        out_specs=(P(None, split), P(None, split)),
        check_vma=False,
    )
```

```python
import jax
import jax.numpy as jnp
from jax import lax
from jax.experimental import pallas as pl
from jax.experimental.pallas import tpu as pltpu
from jax.sharding import PartitionSpec as P


M_DEV = 512
BLOCK = 512
VMEM_LIMIT = 16 << 20

eps = 1e-05
bf16 = jnp.bfloat16
f32 = jnp.float32


def contract(left, right, left_dim, right_dim):
    return lax.dot_general(
        left, right, (((left_dim,), (right_dim,)), ((), ())), preferred_element_type=f32
    )


def nn(left, right):
    return contract(left, right, 1, 0)


def nt(left, right):
    return contract(left, right, 1, 1)


def tn(left, right):
    return contract(left, right, 0, 0)


def swish(values):
    half = values * 0.5
    return half * jnp.tanh(half) + half


def norm_columns(values, gain):
    count = 1.0 / values.shape[0]
    mean = jnp.sum(values, axis=0, keepdims=True) * count
    var = jnp.sum(values * values, axis=0, keepdims=True) * count - mean * mean
    return (values - mean) * lax.rsqrt(var + eps) * gain


def pick_rows(index_row, count):
    rows = lax.broadcasted_iota(jnp.int16, (count, index_row.shape[1]), 0)
    return jnp.where(rows == index_row.astype(jnp.int16), bf16(1), bf16(0))


def pick_columns(index_column, count):
    columns = lax.broadcasted_iota(jnp.int16, (index_column.shape[0], count), 1)
    return jnp.where(columns == index_column.astype(jnp.int16), bf16(1), bf16(0))


def blocks(total):
    return [pl.ds(start, BLOCK) for start in range(0, total, BLOCK)]


def embed_columns(x, embed_w, second_w, bias, gain):
    hidden = swish(tn(embed_w, x) + bias).astype(bf16)
    return norm_columns(nn(second_w, hidden), gain).astype(bf16)


class Fetch:
    def __init__(self, source, buffer, semaphore):
        self.copy = pltpu.make_async_copy(source, buffer, semaphore)
        self.copy.start()
        self.buffer = buffer
        self.arrived = False

    def __call__(self):
        if not self.arrived:
            self.copy.wait()
            self.arrived = True
        return self.buffer


def column(rows, i):
    return jnp.transpose(rows[...])[:, i : i + 1]


def index_row(index, part):
    return index[part].reshape(1, -1)


def outside(index, count, reach):
    beyond = jnp.where(index >= count, index - count + reach, -1)
    return jnp.where(index < 0, index + reach, beyond)


def index_column(index, part):
    row = index_row(index, part).astype(f32)
    return jnp.transpose(jnp.broadcast_to(row, (8, row.shape[1])))[:, :1].astype(jnp.int32)


def place():
    return lax.axis_index("space") * lax.axis_size("chan") + lax.axis_index("chan")


def embed_kernel(
    x,
    embed_w,
    biases,
    second_w,
    gains,
    send_w,
    send_index,
    geom,
    geom_w,
    recv_index,
    rows,
    latent,
    own_terms,
    sums,
    picks,
    table,
):
    bias = column(biases(), 0)
    cells = x().shape[1]
    nodes = sums.shape[0]
    for part in blocks(cells):
        hidden = swish(tn(embed_w()[...], x()[:, part]) + bias).astype(bf16)
        values = norm_columns(nn(second_w()[...], hidden), column(gains(), 0)).astype(bf16)
        latent[:, part] = values
        table[:, part] = nn(send_w()[...], values).astype(bf16)
    bias = column(biases(), 1)
    for part in blocks(geom().shape[1]):
        own = index_row(send_index(), part) - place() * cells
        terms = nn(table[...], pick_rows(own, cells))
        own_terms[:, part] = terms + tn(geom_w()[...], geom()[:, part]) + bias
        sums[:, part] = pick_rows(index_row(recv_index(), part) - place() * nodes, nodes)
    row_columns = jnp.transpose(rows()[...].astype(f32)).astype(jnp.int32)
    per_row, count = row_columns.shape
    for i in range(count):
        picks[i * per_row : (i + 1) * per_row, :] = pick_columns(row_columns[:, i : i + 1], nodes)


def encode_kernel(
    grid_latent,
    own_terms,
    sums,
    picks,
    low,
    high,
    embed_w,
    embed_second_w,
    send_w,
    biases,
    gains,
    send_index,
    edge_w,
    link_w,
    grid_latent_out,
    latent,
    outgoing,
    messages,
    staged,
    nodes_near,
    semaphores,
):
    copies = [pltpu.make_async_copy(grid_latent, grid_latent_out, semaphores.at[0])]
    copies[0].start()
    halo = jnp.concatenate([low[...], high[...]], axis=1)
    reach = halo.shape[1] // 2
    cells = grid_latent.shape[1]
    halo = embed_columns(
        halo, embed_w[...], embed_second_w[...], column(biases, 0), column(gains, 0)
    )
    halo = nn(send_w[...], halo).astype(bf16)
    gain = column(gains, 1)
    for part in blocks(own_terms.shape[1]):
        index = outside(index_row(send_index, part) - place() * cells, cells, reach)
        pre_act = own_terms[:, part] + nn(halo, pick_rows(index, 2 * reach))
        hidden = swish(pre_act).astype(bf16)
        messages[:, part] = norm_columns(nn(edge_w[...], hidden), gain).astype(bf16)
    nodes = nt(sums[...], messages[...]).astype(bf16)
    nodes_near[...] = nodes
    copies.append(pltpu.make_async_copy(nodes_near, latent, semaphores.at[1]))
    copies[-1].start()
    link = nt(nodes, link_w[...]).astype(bf16)
    for part in blocks(outgoing.shape[0]):
        staged[part, :] = nn(picks[part, :], link).astype(bf16)
        copies.append(
            pltpu.make_async_copy(
                staged.at[part, :], outgoing.at[part, :], semaphores.at[len(copies)]
            )
        )
        copies[-1].start()
    for copy in copies:
        copy.wait()


def window_kernel(
    latent,
    mesh_geom,
    recv_w,
    biases,
    mesh_geom_w,
    recv_index,
    node_w,
    grid_latent,
    decode_w,
    out_w,
    cell_geom_w,
    cell_geom,
    recv_terms,
    node_terms,
    latent_columns,
    cell_terms,
    out_terms,
):
    nodes = latent()[...]
    recv_bias = biases()[2:3, :]
    for part in blocks(recv_terms.shape[0]):
        picked = index_column(recv_index(), part) - place() * nodes.shape[0]
        picked = pick_columns(picked, nodes.shape[0])
        picked = nn(picked, nodes).astype(bf16)
        terms = nt(picked, recv_w()[...]) + tn(mesh_geom()[:, part], mesh_geom_w()[...])
        recv_terms[part, :] = terms + recv_bias
    node_terms[...] = nt(node_w()[...], nodes) + column(biases(), 3)
    latent_columns[...] = jnp.transpose(nodes.astype(f32)).astype(bf16)
    cell_bias = column(biases(), 4)
    out_bias = column(biases(), 5)
    for part in blocks(grid_latent().shape[1]):
        cells = grid_latent()[:, part]
        out_terms[:, part] = nn(out_w()[...], cells) + out_bias
        terms = nn(decode_w()[...], cells) + cell_bias
        for k in range(cell_terms.shape[0]):
            cell_terms[k, :, part] = terms + tn(cell_geom_w()[...], cell_geom()[k, :, part])


def mesh_kernel(edge_w, *refs):
    *recv_terms, node_w, node_terms, node_second_w, latent_columns, send_w = refs[:-12]
    slot_index, recv_index, gains = refs[-12:-9]
    arrived, state, send, send_low, send_high = refs[-9:-4]
    messages, gathered, staged, semaphore = refs[-4:]
    reach = send_low.shape[1]
    count = state.shape[1]
    parts = blocks(messages.shape[1])
    gain = column(gains, 2)
    ahead = 2
    sums = []
    for i in range(len(parts) + ahead):
        if i < len(parts):
            picks = pick_columns(index_column(slot_index, parts[i]), arrived.shape[0])
            gathered[parts[i], :] = nn(picks, arrived[...])
        if i >= ahead:
            part = parts[i - ahead]
            hidden = swish(gathered[part, :] + recv_terms[i - ahead]()[...]).astype(bf16)
            messages[:, part] = norm_columns(nt(edge_w()[...], hidden), gain).astype(bf16)
            index = index_row(recv_index, part) - place() * count
            sums.append(pick_rows(index, count))
    nodes = nt(jnp.concatenate(sums, axis=1), messages[...]).astype(bf16)
    hidden = swish(nt(node_w()[...], nodes) + node_terms()[...]).astype(bf16)
    normed = norm_columns(nn(node_second_w()[...], hidden), column(gains, 3))
    values = (latent_columns()[...].astype(f32) + normed).astype(bf16)
    staged[...] = values
    copy = pltpu.make_async_copy(staged, state, semaphore)
    copy.start()
    sent = nn(send_w()[...], values).astype(bf16)
    send[...] = sent
    send_low[...] = sent[:, :reach]
    send_high[...] = sent[:, sent.shape[1] - reach :]
    copy.wait()


def local_kernel(index, *refs):
    *terms, send, out = refs
    for k in range(out.shape[0]):
        for part in blocks(out.shape[2]):
            picks = index()[k, :, part] - place() * send.shape[1]
            picks = pick_rows(picks, send.shape[1])
            out[k, :, part] = terms[k]()[:, part] + nn(send[...], picks)


def decode_kernel(
    low,
    high,
    index,
    terms,
    edge_w,
    gains,
    gathered_w,
    out_terms,
    out_w,
    out_bias,
    prediction,
    staged,
    semaphores,
):
    halo = jnp.concatenate([low[...], high[...]], axis=1)
    gain = column(gains, 4)
    offset = out_bias[...].reshape(1, -1)
    offset = jnp.transpose(jnp.broadcast_to(offset, (8, offset.shape[1])))[:, :1]
    copies = []
    for part in blocks(terms.shape[2]):
        total = None
        for k in range(terms.shape[0]):
            count = 2 * halo.shape[1]
            picks = outside(index[k, :, part] - place() * count, count, halo.shape[1] // 2)
            picks = pick_rows(picks, halo.shape[1])
            hidden = swish(terms[k, :, part] + nn(halo, picks)).astype(bf16)
            message = norm_columns(nn(edge_w[...], hidden), gain).astype(bf16).astype(f32)
            total = message if total is None else total + message
        pre_act = out_terms[:, part] + nn(gathered_w[...], total.astype(bf16))
        hidden = swish(pre_act).astype(bf16)
        staged[:, part] = nn(out_w[...], hidden) + offset
        copies.append(
            pltpu.make_async_copy(
                staged.at[:, part], prediction.at[:, part], semaphores.at[len(copies)]
            )
        )
        copies[-1].start()
    for copy in copies:
        copy.wait()


def part_shape(shape, index):
    lead = tuple(part.size for part in index if isinstance(part, pl.Slice))
    return lead + shape[len(index) :]


def fetching(
    kernel,
    outs,
    fetched=(),
    resident=(),
    carried=(),
    scratch=(),
    in_place=(),
    limit=VMEM_LIMIT,
):
    pairs = [item if isinstance(item, tuple) else (item, ()) for item in fetched]
    n_in, n_res, n_out = len(pairs), len(resident), len(outs)
    extra = []
    for item in carried:
        if isinstance(item, int):
            extra.append(item)
        else:
            pairs.append(item if isinstance(item, tuple) else (item, ()))
            extra.append(len(pairs) - 1)
    arrays = [array for array, _ in pairs]
    shapes = [(part_shape(array.shape, index), array.dtype) for array, index in pairs]
    local = [i for i in range(len(pairs)) if i not in extra]

    def run(*refs):
        sources, refs = refs[: len(pairs)], refs[len(pairs) :]
        near, refs = refs[:n_res], refs[n_res:]
        results, refs = refs[:n_out], refs[n_out:]
        passed, refs = refs[: len(extra)], refs[len(extra) :]
        buffers = dict(zip(extra, passed))
        buffers.update(zip(local, refs[: len(local)]))
        refs = refs[len(local) :]
        copies = []
        if pairs:
            for i, (source, (_, index)) in enumerate(zip(sources, pairs)):
                source = source.at[index] if index else source
                copies.append(Fetch(source, buffers[i], refs[0].at[i]))
            refs = refs[1:]
        kernel(*copies[:n_in], *near, *results, *refs)
        for copy in copies:
            copy()

    near = pl.BlockSpec(memory_space=pltpu.VMEM)
    far = pl.BlockSpec(memory_space=pltpu.HBM)
    return pl.pallas_call(
        run,
        out_shape=tuple(outs) + tuple(pltpu.VMEM(*shapes[i]) for i in extra),
        in_specs=[far] * len(pairs) + [near] * n_res,
        out_specs=tuple(far if i in in_place else near for i in range(n_out))
        + (near,) * len(extra),
        scratch_shapes=[pltpu.VMEM(*shapes[i]) for i in local]
        + ([pltpu.SemaphoreType.DMA((len(pairs),))] if pairs else [])
        + list(scratch),
        compiler_params=pltpu.CompilerParams(vmem_limit_bytes=limit),
    )(
        *[pltpu.with_memory_space_constraint(value, pltpu.HBM) for value in arrays],
        *[pltpu.with_memory_space_constraint(value, pltpu.VMEM) for value in resident],
    )


def exchange(low_end, high_end):
    axes = ("space", "chan")
    count = lax.axis_size("space") * lax.axis_size("chan")
    up = [(i, (i + 1) % count) for i in range(count)]
    down = [(target, source) for source, target in up]
    low = lax.ppermute(high_end, axes, up)
    high = lax.ppermute(low_end, axes, down)
    return low, high


def body(
    grid_in,
    grid_embed_w,
    g2m_w,
    pair_w,
    second_w,
    first_b,
    norm_gain,
    geom_w,
    out_w,
    out_b,
    g2m_geom,
    mesh_geom,
    m2g_geom,
    g2m_send,
    g2m_recv,
    mesh_recv,
    mesh_slot,
    mesh_rows,
    m2g_send,
):
    width = grid_embed_w.shape[0]
    cells = grid_in.shape[1]
    reach = cells // 4
    low, high = exchange(grid_in[:, :reach], grid_in[:, cells - reach :])

    kept = pltpu.VMEM
    shape = pltpu.HBM
    embed_t = grid_embed_w.T
    geom_t = geom_w.transpose(0, 2, 1)
    edges = g2m_geom.shape[1]
    slots = mesh_rows.size
    (
        grid_latent,
        own_terms,
        sums,
        picks,
        embed_near,
        embed_second_near,
        g2m_near,
        bias_near,
        gain_near,
        send_near,
        edge_near,
        link_near,
    ) = fetching(
        embed_kernel,
        (
            kept((width, cells), bf16),
            kept((width, edges), f32),
            kept((M_DEV, edges), bf16),
            kept((slots, M_DEV), bf16),
        ),
        [
            grid_in,
            embed_t,
            first_b,
            (second_w, (0,)),
            norm_gain,
            g2m_w,
            g2m_send,
            g2m_geom,
            (geom_t, (0,)),
            g2m_recv,
            mesh_rows,
        ],
        carried=[1, 3, 5, 2, 4, 6, (second_w, (1,)), (pair_w, (0, 0))],
        scratch=[pltpu.VMEM((width, cells), bf16)],
    )

    grid_latent, latent, outgoing = fetching(
        encode_kernel,
        (
            shape((width, cells), bf16),
            shape((M_DEV, width), bf16),
            shape((slots, width), bf16),
        ),
        resident=[
            grid_latent,
            own_terms,
            sums,
            picks,
            low,
            high,
            embed_near,
            embed_second_near,
            g2m_near,
            bias_near,
            gain_near,
            send_near,
            edge_near,
            link_near,
        ],
        scratch=[
            pltpu.VMEM((width, edges), bf16),
            pltpu.VMEM((slots, width), bf16),
            pltpu.VMEM((M_DEV, width), bf16),
            pltpu.SemaphoreType.DMA((2 + slots // BLOCK,)),
        ],
        in_place=(0, 1, 2),
    )
    arrived = lax.all_to_all(
        outgoing.reshape(mesh_rows.shape + (width,)),
        ("space", "chan"),
        split_axis=0,
        concat_axis=0,
        tiled=True,
    ).reshape(-1, width)

    mesh_edges = mesh_geom.shape[1]
    mesh_reach = M_DEV // 4
    per_cell = m2g_send.shape[0] // cells
    cell_geom = m2g_geom.reshape(-1, cells, per_cell).transpose(2, 0, 1)
    cell_send = m2g_send.reshape(cells, per_cell).T[:, None, :]
    latent, cell_send = lax.optimization_barrier((latent, cell_send))
    recv_terms, node_terms, latent_columns, cell_terms, out_terms = fetching(
        window_kernel,
        (
            shape((mesh_edges, width), f32),
            shape((width, M_DEV), f32),
            shape((width, M_DEV), bf16),
            shape((per_cell, width, cells), f32),
            shape((width, cells), f32),
        ),
        [
            latent,
            mesh_geom,
            (pair_w, (0, 1)),
            first_b,
            (geom_t, (1,)),
            mesh_recv,
            (pair_w, (1, 0)),
            grid_latent,
            (pair_w, (2, 1)),
            (pair_w, (3, 0)),
            (geom_t, (2,)),
            cell_geom,
        ],
        limit=40 << 20,
    )

    state, send, send_low, send_high = fetching(
        mesh_kernel,
        (
            shape((width, M_DEV), bf16),
            kept((width, M_DEV), bf16),
            kept((width, mesh_reach), bf16),
            kept((width, mesh_reach), bf16),
        ),
        [(second_w, (2,))]
        + [(recv_terms, (part,)) for part in blocks(mesh_edges)]
        + [
            (pair_w, (1, 1)),
            node_terms,
            (second_w, (3,)),
            latent_columns,
            (pair_w, (2, 0)),
        ],
        resident=[mesh_slot, mesh_recv, norm_gain, arrived],
        scratch=[
            pltpu.VMEM((width, mesh_edges), bf16),
            pltpu.VMEM((mesh_edges, width), f32),
            pltpu.VMEM((width, M_DEV), bf16),
            pltpu.SemaphoreType.DMA(()),
        ],
        in_place=(0,),
        limit=32 << 20,
    )
    low, high = exchange(send_low, send_high)
    (
        cell_terms,
        send_near,
        decode_near,
        gain_near,
        gathered_near,
        out_terms,
        out_w_near,
        out_b_near,
    ) = fetching(
        local_kernel,
        (kept(cell_terms.shape, f32),),
        [cell_send] + [(cell_terms, (k,)) for k in range(per_cell)],
        resident=[send],
        carried=[
            0,
            (second_w, (4,)),
            norm_gain,
            (pair_w, (3, 1)),
            out_terms,
            out_w,
            out_b,
        ],
    )
    (prediction,) = fetching(
        decode_kernel,
        (shape((out_w.shape[0], cells), f32),),
        resident=[
            low,
            high,
            send_near,
            cell_terms,
            decode_near,
            gain_near,
            gathered_near,
            out_terms,
            out_w_near,
            out_b_near,
        ],
        scratch=[
            pltpu.VMEM((out_w.shape[0], cells), f32),
            pltpu.SemaphoreType.DMA((cells // BLOCK,)),
        ],
        in_place=(0,),
    )
    return (prediction, state)


def solution(mesh):
    split = ("space", "chan")
    return jax.shard_map(
        body,
        mesh=mesh,
        in_specs=(
            P(None, split),
            P(),
            P(),
            P(),
            P(),
            P(),
            P(),
            P(),
            P(),
            P(),
            P(None, split),
            P(None, split),
            P(None, split),
            P(split),
            P(split),
            P(split),
            P(split),
            P(split, None),
            P(split),
        ),
        out_specs=(P(None, split), P(None, split)),
        check_vma=False,
    )
```

```python
import jax
import jax.numpy as jnp
from jax import lax
from jax.experimental import pallas as pl
from jax.experimental.pallas import tpu as pltpu
from jax.sharding import PartitionSpec as P


M_DEV = 512
BLOCK = 512
VMEM_LIMIT = 16 << 20

eps = 1e-05
bf16 = jnp.bfloat16
f32 = jnp.float32


def contract(left, right, left_dim, right_dim):
    return lax.dot_general(
        left, right, (((left_dim,), (right_dim,)), ((), ())), preferred_element_type=f32
    )


def nn(left, right):
    return contract(left, right, 1, 0)


def nt(left, right):
    return contract(left, right, 1, 1)


def tn(left, right):
    return contract(left, right, 0, 0)


def swish(values):
    return swish_of_half(values * 0.5)


def swish_of_half(half):
    return half * jnp.tanh(half) + half


def norm_columns(values, gain):
    count = 1.0 / values.shape[0]
    mean = jnp.sum(values, axis=0, keepdims=True) * count
    var = jnp.sum(values * values, axis=0, keepdims=True) * count - mean * mean
    return (values - mean) * lax.rsqrt(var + eps) * gain


def pick_rows(index_row, count, value=1):
    rows = lax.broadcasted_iota(jnp.int16, (count, index_row.shape[1]), 0)
    return jnp.where(rows == index_row.astype(jnp.int16), bf16(value), bf16(0))


def pick_columns(index_column, count, value=1):
    columns = lax.broadcasted_iota(jnp.int16, (index_column.shape[0], count), 1)
    return jnp.where(columns == index_column.astype(jnp.int16), bf16(value), bf16(0))


def blocks(total):
    return [pl.ds(start, BLOCK) for start in range(0, total, BLOCK)]


def embed_columns(x, embed_w, second_w, bias, gain):
    hidden = swish(tn(embed_w, x) + bias).astype(bf16)
    return norm_columns(nn(second_w, hidden), gain).astype(bf16)


class Fetch:
    def __init__(self, source, buffer, semaphore):
        self.copy = pltpu.make_async_copy(source, buffer, semaphore)
        self.copy.start()
        self.buffer = buffer
        self.arrived = False

    def __call__(self):
        if not self.arrived:
            self.copy.wait()
            self.arrived = True
        return self.buffer


def column(rows, i):
    return jnp.transpose(rows[...])[:, i : i + 1]


def index_row(index, part):
    return index[part].reshape(1, -1)


def outside(index, count, reach):
    beyond = jnp.where(index >= count, index - count + reach, -1)
    return jnp.where(index < 0, index + reach, beyond)


def index_column(index, part):
    row = index_row(index, part).astype(f32)
    return jnp.transpose(jnp.broadcast_to(row, (8, row.shape[1])))[:, :1].astype(jnp.int32)


def stagger(parts, first, second):
    waiting = None
    for part in parts:
        values = first(part)
        if waiting is not None:
            second(*waiting)
        waiting = (part, values)
    second(*waiting)


def place():
    return lax.axis_index("space") * lax.axis_size("chan") + lax.axis_index("chan")


def embed_kernel(
    x,
    embed_w,
    biases,
    second_w,
    gains,
    send_w,
    send_index,
    geom,
    geom_w,
    recv_index,
    rows,
    latent,
    own_terms,
    sums,
    picks,
    table,
):
    bias = column(biases(), 0)
    cells = x().shape[1]
    nodes = sums.shape[0]
    for part in blocks(cells):
        hidden = swish(tn(embed_w()[...], x()[:, part]) + bias).astype(bf16)
        values = norm_columns(nn(second_w()[...], hidden), column(gains(), 0)).astype(bf16)
        latent[:, part] = values
        table[:, part] = nn(send_w()[...], values).astype(bf16)
    bias = column(biases(), 1) * 0.5
    half_w = geom_w()[...] * bf16(0.5)
    for part in blocks(geom().shape[1]):
        own = index_row(send_index(), part) - place() * cells
        terms = nn(table[...], pick_rows(own, cells, 0.5))
        own_terms[:, part] = terms + tn(half_w, geom()[:, part]) + bias
        sums[:, part] = pick_rows(index_row(recv_index(), part) - place() * nodes, nodes)
    row_columns = jnp.transpose(rows()[...].astype(f32)).astype(jnp.int32)
    per_row, count = row_columns.shape
    for i in range(count):
        picks[i * per_row : (i + 1) * per_row, :] = pick_columns(row_columns[:, i : i + 1], nodes)


def encode_kernel(
    grid_latent,
    own_terms,
    sums,
    picks,
    low,
    high,
    embed_w,
    embed_second_w,
    send_w,
    biases,
    gains,
    send_index,
    edge_w,
    link_w,
    grid_latent_out,
    latent,
    outgoing,
    messages,
    staged,
    nodes_near,
    semaphores,
):
    copies = [pltpu.make_async_copy(grid_latent, grid_latent_out, semaphores.at[0])]
    copies[0].start()
    halo = jnp.concatenate([low[...], high[...]], axis=1)
    reach = halo.shape[1] // 2
    cells = grid_latent.shape[1]
    halo = embed_columns(
        halo, embed_w[...], embed_second_w[...], column(biases, 0), column(gains, 0)
    )
    halo = nn(send_w[...], halo).astype(bf16)
    gain = column(gains, 1)

    def first(part):
        index = outside(index_row(send_index, part) - place() * cells, cells, reach)
        half = own_terms[:, part] + nn(halo, pick_rows(index, 2 * reach, 0.5))
        return nn(edge_w[...], swish_of_half(half).astype(bf16))

    def second(part, values):
        messages[:, part] = norm_columns(values, gain).astype(bf16)

    stagger(blocks(own_terms.shape[1]), first, second)
    nodes = nt(sums[...], messages[...]).astype(bf16)
    nodes_near[...] = nodes
    copies.append(pltpu.make_async_copy(nodes_near, latent, semaphores.at[1]))
    copies[-1].start()
    link = nt(nodes, link_w[...]).astype(bf16)
    for part in blocks(outgoing.shape[0]):
        staged[part, :] = nn(picks[part, :], link).astype(bf16)
        copies.append(
            pltpu.make_async_copy(
                staged.at[part, :], outgoing.at[part, :], semaphores.at[len(copies)]
            )
        )
        copies[-1].start()
    for copy in copies:
        copy.wait()


def window_kernel(
    latent,
    mesh_geom,
    recv_w,
    biases,
    mesh_geom_w,
    recv_index,
    node_w,
    grid_latent,
    decode_w,
    out_w,
    cell_geom_w,
    cell_geom,
    recv_terms,
    node_terms,
    latent_columns,
    cell_terms,
    out_terms,
):
    nodes = latent()[...]
    recv_bias = biases()[2:3, :]
    for part in blocks(recv_terms.shape[0]):
        picked = index_column(recv_index(), part) - place() * nodes.shape[0]
        picked = pick_columns(picked, nodes.shape[0])
        picked = nn(picked, nodes).astype(bf16)
        terms = nt(picked, recv_w()[...]) + tn(mesh_geom()[:, part], mesh_geom_w()[...])
        recv_terms[part, :] = (terms + recv_bias) * 0.5
    node_terms[...] = nt(node_w()[...], nodes) + column(biases(), 3)
    latent_columns[...] = jnp.transpose(nodes.astype(f32)).astype(bf16)
    cell_bias = column(biases(), 4)
    out_bias = column(biases(), 5)
    for part in blocks(grid_latent().shape[1]):
        cells = grid_latent()[:, part]
        out_terms[:, part] = nn(out_w()[...], cells) + out_bias
        terms = nn(decode_w()[...], cells) + cell_bias
        for k in range(cell_terms.shape[0]):
            whole = terms + tn(cell_geom_w()[...], cell_geom()[k, :, part])
            cell_terms[k, :, part] = whole * 0.5


def mesh_kernel(edge_w, *refs):
    *recv_terms, node_w, node_terms, node_second_w, latent_columns, send_w = refs[:-12]
    slot_index, recv_index, gains = refs[-12:-9]
    arrived, state, send, send_low, send_high = refs[-9:-4]
    messages, gathered, staged, semaphore = refs[-4:]
    reach = send_low.shape[1]
    count = state.shape[1]
    parts = blocks(messages.shape[1])
    gain = column(gains, 2)
    ahead = 2
    sums = []
    for i in range(len(parts) + ahead):
        if i < len(parts):
            picks = pick_columns(index_column(slot_index, parts[i]), arrived.shape[0], 0.5)
            gathered[parts[i], :] = nn(picks, arrived[...])
        if i >= ahead:
            part = parts[i - ahead]
            half = gathered[part, :] + recv_terms[i - ahead]()[...]
            hidden = swish_of_half(half).astype(bf16)
            messages[:, part] = norm_columns(nt(edge_w()[...], hidden), gain).astype(bf16)
            index = index_row(recv_index, part) - place() * count
            sums.append(pick_rows(index, count))
    nodes = nt(jnp.concatenate(sums, axis=1), messages[...]).astype(bf16)
    hidden = swish(nt(node_w()[...], nodes) + node_terms()[...]).astype(bf16)
    normed = norm_columns(nn(node_second_w()[...], hidden), column(gains, 3))
    values = (latent_columns()[...].astype(f32) + normed).astype(bf16)
    staged[...] = values
    copy = pltpu.make_async_copy(staged, state, semaphore)
    copy.start()
    sent = nn(send_w()[...], values).astype(bf16)
    send[...] = sent
    send_low[...] = sent[:, :reach]
    send_high[...] = sent[:, sent.shape[1] - reach :]
    copy.wait()


def local_kernel(index, *refs):
    *terms, send, out = refs
    for k in range(out.shape[0]):
        for part in blocks(out.shape[2]):
            picks = index()[k, :, part] - place() * send.shape[1]
            picks = pick_rows(picks, send.shape[1], 0.5)
            out[k, :, part] = terms[k]()[:, part] + nn(send[...], picks)


def decode_kernel(
    low,
    high,
    index,
    terms,
    edge_w,
    gains,
    gathered_w,
    out_terms,
    out_w,
    out_bias,
    prediction,
    staged,
    semaphores,
):
    halo = jnp.concatenate([low[...], high[...]], axis=1)
    gain = column(gains, 4)
    offset = out_bias[...].reshape(1, -1)
    offset = jnp.transpose(jnp.broadcast_to(offset, (8, offset.shape[1])))[:, :1]
    copies = []
    totals = {}
    last = terms.shape[0] - 1

    def first(spot):
        part, k = spot
        count = 2 * halo.shape[1]
        picks = outside(index[k, :, part] - place() * count, count, halo.shape[1] // 2)
        half = terms[k, :, part] + nn(halo, pick_rows(picks, halo.shape[1], 0.5))
        return nn(edge_w[...], swish_of_half(half).astype(bf16))

    def second(spot, values):
        part, k = spot
        message = norm_columns(values, gain).astype(bf16).astype(f32)
        totals[part.start] = message if k == 0 else totals[part.start] + message
        if k < last:
            return
        total = totals[part.start].astype(bf16)
        pre_act = out_terms[:, part] + nn(gathered_w[...], total)
        hidden = swish(pre_act).astype(bf16)
        staged[:, part] = nn(out_w[...], hidden) + offset
        copies.append(
            pltpu.make_async_copy(
                staged.at[:, part], prediction.at[:, part], semaphores.at[len(copies)]
            )
        )
        copies[-1].start()

    spots = [(part, k) for part in blocks(terms.shape[2]) for k in range(last + 1)]
    stagger(spots, first, second)
    for copy in copies:
        copy.wait()


def part_shape(shape, index):
    lead = tuple(part.size for part in index if isinstance(part, pl.Slice))
    return lead + shape[len(index) :]


def fetching(
    kernel,
    outs,
    fetched=(),
    resident=(),
    carried=(),
    scratch=(),
    in_place=(),
    limit=VMEM_LIMIT,
):
    pairs = [item if isinstance(item, tuple) else (item, ()) for item in fetched]
    n_in, n_res, n_out = len(pairs), len(resident), len(outs)
    extra = []
    for item in carried:
        if isinstance(item, int):
            extra.append(item)
        else:
            pairs.append(item if isinstance(item, tuple) else (item, ()))
            extra.append(len(pairs) - 1)
    arrays = [array for array, _ in pairs]
    shapes = [(part_shape(array.shape, index), array.dtype) for array, index in pairs]
    local = [i for i in range(len(pairs)) if i not in extra]

    def run(*refs):
        sources, refs = refs[: len(pairs)], refs[len(pairs) :]
        near, refs = refs[:n_res], refs[n_res:]
        results, refs = refs[:n_out], refs[n_out:]
        passed, refs = refs[: len(extra)], refs[len(extra) :]
        buffers = dict(zip(extra, passed))
        buffers.update(zip(local, refs[: len(local)]))
        refs = refs[len(local) :]
        copies = []
        if pairs:
            for i, (source, (_, index)) in enumerate(zip(sources, pairs)):
                source = source.at[index] if index else source
                copies.append(Fetch(source, buffers[i], refs[0].at[i]))
            refs = refs[1:]
        kernel(*copies[:n_in], *near, *results, *refs)
        for copy in copies:
            copy()

    near = pl.BlockSpec(memory_space=pltpu.VMEM)
    far = pl.BlockSpec(memory_space=pltpu.HBM)
    return pl.pallas_call(
        run,
        out_shape=tuple(outs) + tuple(pltpu.VMEM(*shapes[i]) for i in extra),
        in_specs=[far] * len(pairs) + [near] * n_res,
        out_specs=tuple(far if i in in_place else near for i in range(n_out))
        + (near,) * len(extra),
        scratch_shapes=[pltpu.VMEM(*shapes[i]) for i in local]
        + ([pltpu.SemaphoreType.DMA((len(pairs),))] if pairs else [])
        + list(scratch),
        compiler_params=pltpu.CompilerParams(vmem_limit_bytes=limit),
    )(
        *[pltpu.with_memory_space_constraint(value, pltpu.HBM) for value in arrays],
        *[pltpu.with_memory_space_constraint(value, pltpu.VMEM) for value in resident],
    )


def exchange(low_end, high_end):
    axes = ("space", "chan")
    count = lax.axis_size("space") * lax.axis_size("chan")
    up = [(i, (i + 1) % count) for i in range(count)]
    down = [(target, source) for source, target in up]
    low = lax.ppermute(high_end, axes, up)
    high = lax.ppermute(low_end, axes, down)
    return low, high


def body(
    grid_in,
    grid_embed_w,
    g2m_w,
    pair_w,
    second_w,
    first_b,
    norm_gain,
    geom_w,
    out_w,
    out_b,
    g2m_geom,
    mesh_geom,
    m2g_geom,
    g2m_send,
    g2m_recv,
    mesh_recv,
    mesh_slot,
    mesh_rows,
    m2g_send,
):
    width = grid_embed_w.shape[0]
    cells = grid_in.shape[1]
    reach = cells // 4
    low, high = exchange(grid_in[:, :reach], grid_in[:, cells - reach :])

    kept = pltpu.VMEM
    shape = pltpu.HBM
    embed_t = grid_embed_w.T
    geom_t = geom_w.transpose(0, 2, 1)
    edges = g2m_geom.shape[1]
    slots = mesh_rows.size
    (
        grid_latent,
        own_terms,
        sums,
        picks,
        embed_near,
        embed_second_near,
        g2m_near,
        bias_near,
        gain_near,
        send_near,
        edge_near,
        link_near,
    ) = fetching(
        embed_kernel,
        (
            kept((width, cells), bf16),
            kept((width, edges), f32),
            kept((M_DEV, edges), bf16),
            kept((slots, M_DEV), bf16),
        ),
        [
            grid_in,
            embed_t,
            first_b,
            (second_w, (0,)),
            norm_gain,
            g2m_w,
            g2m_send,
            g2m_geom,
            (geom_t, (0,)),
            g2m_recv,
            mesh_rows,
        ],
        carried=[1, 3, 5, 2, 4, 6, (second_w, (1,)), (pair_w, (0, 0))],
        scratch=[pltpu.VMEM((width, cells), bf16)],
    )

    grid_latent, latent, outgoing = fetching(
        encode_kernel,
        (
            shape((width, cells), bf16),
            shape((M_DEV, width), bf16),
            shape((slots, width), bf16),
        ),
        resident=[
            grid_latent,
            own_terms,
            sums,
            picks,
            low,
            high,
            embed_near,
            embed_second_near,
            g2m_near,
            bias_near,
            gain_near,
            send_near,
            edge_near,
            link_near,
        ],
        scratch=[
            pltpu.VMEM((width, edges), bf16),
            pltpu.VMEM((slots, width), bf16),
            pltpu.VMEM((M_DEV, width), bf16),
            pltpu.SemaphoreType.DMA((2 + slots // BLOCK,)),
        ],
        in_place=(0, 1, 2),
    )
    arrived = lax.all_to_all(
        outgoing.reshape(mesh_rows.shape + (width,)),
        ("space", "chan"),
        split_axis=0,
        concat_axis=0,
        tiled=True,
    ).reshape(-1, width)

    mesh_edges = mesh_geom.shape[1]
    mesh_reach = M_DEV // 4
    per_cell = m2g_send.shape[0] // cells
    cell_geom = m2g_geom.reshape(-1, cells, per_cell).transpose(2, 0, 1)
    cell_send = m2g_send.reshape(cells, per_cell).T[:, None, :]
    latent, cell_send = lax.optimization_barrier((latent, cell_send))
    recv_terms, node_terms, latent_columns, cell_terms, out_terms = fetching(
        window_kernel,
        (
            shape((mesh_edges, width), f32),
            shape((width, M_DEV), f32),
            shape((width, M_DEV), bf16),
            shape((per_cell, width, cells), f32),
            shape((width, cells), f32),
        ),
        [
            latent,
            mesh_geom,
            (pair_w, (0, 1)),
            first_b,
            (geom_t, (1,)),
            mesh_recv,
            (pair_w, (1, 0)),
            grid_latent,
            (pair_w, (2, 1)),
            (pair_w, (3, 0)),
            (geom_t, (2,)),
            cell_geom,
        ],
        limit=40 << 20,
    )

    state, send, send_low, send_high = fetching(
        mesh_kernel,
        (
            shape((width, M_DEV), bf16),
            kept((width, M_DEV), bf16),
            kept((width, mesh_reach), bf16),
            kept((width, mesh_reach), bf16),
        ),
        [(second_w, (2,))]
        + [(recv_terms, (part,)) for part in blocks(mesh_edges)]
        + [
            (pair_w, (1, 1)),
            node_terms,
            (second_w, (3,)),
            latent_columns,
            (pair_w, (2, 0)),
        ],
        resident=[mesh_slot, mesh_recv, norm_gain, arrived],
        scratch=[
            pltpu.VMEM((width, mesh_edges), bf16),
            pltpu.VMEM((mesh_edges, width), f32),
            pltpu.VMEM((width, M_DEV), bf16),
            pltpu.SemaphoreType.DMA(()),
        ],
        in_place=(0,),
        limit=32 << 20,
    )
    low, high = exchange(send_low, send_high)
    (
        cell_terms,
        send_near,
        decode_near,
        gain_near,
        gathered_near,
        out_terms,
        out_w_near,
        out_b_near,
    ) = fetching(
        local_kernel,
        (kept(cell_terms.shape, f32),),
        [cell_send] + [(cell_terms, (k,)) for k in range(per_cell)],
        resident=[send],
        carried=[
            0,
            (second_w, (4,)),
            norm_gain,
            (pair_w, (3, 1)),
            out_terms,
            out_w,
            out_b,
        ],
    )
    (prediction,) = fetching(
        decode_kernel,
        (shape((out_w.shape[0], cells), f32),),
        resident=[
            low,
            high,
            send_near,
            cell_terms,
            decode_near,
            gain_near,
            gathered_near,
            out_terms,
            out_w_near,
            out_b_near,
        ],
        scratch=[
            pltpu.VMEM((out_w.shape[0], cells), f32),
            pltpu.SemaphoreType.DMA((cells // BLOCK,)),
        ],
        in_place=(0,),
    )
    return (prediction, state)


def solution(mesh):
    split = ("space", "chan")
    return jax.shard_map(
        body,
        mesh=mesh,
        in_specs=(
            P(None, split),
            P(),
            P(),
            P(),
            P(),
            P(),
            P(),
            P(),
            P(),
            P(),
            P(None, split),
            P(None, split),
            P(None, split),
            P(split),
            P(split),
            P(split),
            P(split),
            P(split, None),
            P(split),
        ),
        out_specs=(P(None, split), P(None, split)),
        check_vma=False,
    )
```

```python
import jax
import jax.numpy as jnp
from jax import lax
from jax.experimental import pallas as pl
from jax.experimental.pallas import tpu as pltpu
from jax.sharding import PartitionSpec as P


M_DEV = 512
BLOCK = 512
VMEM_LIMIT = 16 << 20

eps = 1e-05
bf16 = jnp.bfloat16
f32 = jnp.float32


def contract(left, right, left_dim, right_dim):
    return lax.dot_general(
        left, right, (((left_dim,), (right_dim,)), ((), ())), preferred_element_type=f32
    )


def nn(left, right):
    return contract(left, right, 1, 0)


def nt(left, right):
    return contract(left, right, 1, 1)


def tn(left, right):
    return contract(left, right, 0, 0)


def swish(values):
    return swish_of_half(values * 0.5)


def swish_of_half(half):
    return half * jnp.tanh(half) + half


def norm_columns(values, gain):
    count = 1.0 / values.shape[0]
    mean = jnp.sum(values, axis=0, keepdims=True) * count
    var = jnp.sum(values * values, axis=0, keepdims=True) * count - mean * mean
    return (values - mean) * lax.rsqrt(var + eps) * gain


def pick_rows(index_row, count, value=1):
    rows = lax.broadcasted_iota(jnp.int16, (count, index_row.shape[1]), 0)
    return jnp.where(rows == index_row.astype(jnp.int16), bf16(value), bf16(0))


def pick_columns(index_column, count, value=1):
    columns = lax.broadcasted_iota(jnp.int16, (index_column.shape[0], count), 1)
    return jnp.where(columns == index_column.astype(jnp.int16), bf16(value), bf16(0))


def blocks(total):
    return [pl.ds(start, BLOCK) for start in range(0, total, BLOCK)]


def embed_columns(x, embed_w, second_w, bias, gain):
    hidden = swish(tn(embed_w, x) + bias).astype(bf16)
    return norm_columns(nn(second_w, hidden), gain).astype(bf16)


class Fetch:
    def __init__(self, source, buffer, semaphore):
        self.copy = pltpu.make_async_copy(source, buffer, semaphore)
        self.copy.start()
        self.buffer = buffer
        self.arrived = False

    def __call__(self):
        if not self.arrived:
            self.copy.wait()
            self.arrived = True
        return self.buffer


def column(rows, i):
    return jnp.transpose(rows[...])[:, i : i + 1]


def index_row(index, part):
    return index[part].reshape(1, -1)


def outside(index, count, reach):
    beyond = jnp.where(index >= count, index - count + reach, -1)
    return jnp.where(index < 0, index + reach, beyond)


def index_column(index, part):
    row = index_row(index, part).astype(f32)
    return jnp.transpose(jnp.broadcast_to(row, (8, row.shape[1])))[:, :1].astype(jnp.int32)


def stagger(parts, first, second):
    waiting = None
    for part in parts:
        values = first(part)
        if waiting is not None:
            second(*waiting)
        waiting = (part, values)
    second(*waiting)


def place():
    return lax.axis_index("space") * lax.axis_size("chan") + lax.axis_index("chan")


def embed_kernel(
    x,
    embed_w,
    biases,
    second_w,
    gains,
    send_w,
    send_index,
    geom,
    geom_w,
    recv_index,
    rows,
    latent,
    own_terms,
    sums,
    picks,
    table,
):
    bias = column(biases(), 0)
    cells = x().shape[1]
    nodes = sums.shape[0]

    def first(part):
        hidden = swish(tn(embed_w()[...], x()[:, part]) + bias).astype(bf16)
        return nn(second_w()[...], hidden)

    def second(part, values):
        values = norm_columns(values, column(gains(), 0)).astype(bf16)
        latent[:, part] = values
        table[:, part] = nn(send_w()[...], values).astype(bf16)

    stagger(blocks(cells), first, second)
    edge_bias = column(biases(), 1) * 0.5
    half_w = geom_w()[...] * bf16(0.5)
    for part in blocks(geom().shape[1]):
        own = index_row(send_index(), part) - place() * cells
        terms = nn(table[...], pick_rows(own, cells, 0.5))
        own_terms[:, part] = terms + tn(half_w, geom()[:, part]) + edge_bias
        sums[:, part] = pick_rows(index_row(recv_index(), part) - place() * nodes, nodes)
    row_columns = jnp.transpose(rows()[...].astype(f32)).astype(jnp.int32)
    per_row, count = row_columns.shape
    for i in range(count):
        picks[i * per_row : (i + 1) * per_row, :] = pick_columns(row_columns[:, i : i + 1], nodes)


def encode_kernel(
    grid_latent,
    own_terms,
    sums,
    picks,
    low,
    high,
    embed_w,
    embed_second_w,
    send_w,
    biases,
    gains,
    send_index,
    edge_w,
    link_w,
    grid_latent_out,
    latent,
    outgoing,
    messages,
    staged,
    nodes_near,
    semaphores,
):
    copies = [pltpu.make_async_copy(grid_latent, grid_latent_out, semaphores.at[0])]
    copies[0].start()
    halo = jnp.concatenate([low[...], high[...]], axis=1)
    reach = halo.shape[1] // 2
    cells = grid_latent.shape[1]
    halo = embed_columns(
        halo, embed_w[...], embed_second_w[...], column(biases, 0), column(gains, 0)
    )
    halo = nn(send_w[...], halo).astype(bf16)
    gain = column(gains, 1)

    def first(part):
        index = outside(index_row(send_index, part) - place() * cells, cells, reach)
        half = own_terms[:, part] + nn(halo, pick_rows(index, 2 * reach, 0.5))
        return nn(edge_w[...], swish_of_half(half).astype(bf16))

    def second(part, values):
        messages[:, part] = norm_columns(values, gain).astype(bf16)

    stagger(blocks(own_terms.shape[1]), first, second)
    nodes = nt(sums[...], messages[...]).astype(bf16)
    nodes_near[...] = nodes
    copies.append(pltpu.make_async_copy(nodes_near, latent, semaphores.at[1]))
    copies[-1].start()
    link = nt(nodes, link_w[...]).astype(bf16)
    for part in blocks(outgoing.shape[0]):
        staged[part, :] = nn(picks[part, :], link).astype(bf16)
        copies.append(
            pltpu.make_async_copy(
                staged.at[part, :], outgoing.at[part, :], semaphores.at[len(copies)]
            )
        )
        copies[-1].start()
    for copy in copies:
        copy.wait()


def window_kernel(
    latent,
    mesh_geom,
    recv_w,
    biases,
    mesh_geom_w,
    recv_index,
    node_w,
    grid_latent,
    decode_w,
    out_w,
    cell_geom_w,
    cell_geom,
    recv_terms,
    node_terms,
    latent_columns,
    cell_terms,
    out_terms,
):
    nodes = latent()[...]
    recv_bias = biases()[2:3, :]
    for part in blocks(recv_terms.shape[0]):
        picked = index_column(recv_index(), part) - place() * nodes.shape[0]
        picked = pick_columns(picked, nodes.shape[0])
        picked = nn(picked, nodes).astype(bf16)
        terms = nt(picked, recv_w()[...]) + tn(mesh_geom()[:, part], mesh_geom_w()[...])
        recv_terms[part, :] = (terms + recv_bias) * 0.5
    node_terms[...] = nt(node_w()[...], nodes) + column(biases(), 3)
    latent_columns[...] = jnp.transpose(nodes.astype(f32)).astype(bf16)
    cell_bias = column(biases(), 4)
    out_bias = column(biases(), 5)
    for part in blocks(grid_latent().shape[1]):
        cells = grid_latent()[:, part]
        out_terms[:, part] = nn(out_w()[...], cells) + out_bias
        terms = nn(decode_w()[...], cells) + cell_bias
        for k in range(cell_terms.shape[0]):
            whole = terms + tn(cell_geom_w()[...], cell_geom()[k, :, part])
            cell_terms[k, :, part] = whole * 0.5


def mesh_kernel(edge_w, *refs):
    *recv_terms, node_w, node_terms, node_second_w, latent_columns, send_w = refs[:-12]
    slot_index, recv_index, gains = refs[-12:-9]
    arrived, state, send, send_low, send_high = refs[-9:-4]
    messages, gathered, staged, semaphore = refs[-4:]
    reach = send_low.shape[1]
    count = state.shape[1]
    parts = blocks(messages.shape[1])
    gain = column(gains, 2)
    ahead = 2
    waiting = None
    sums = []
    for i in range(len(parts) + ahead):
        if i < len(parts):
            picks = pick_columns(index_column(slot_index, parts[i]), arrived.shape[0], 0.5)
            gathered[parts[i], :] = nn(picks, arrived[...])
        if i >= ahead:
            part = parts[i - ahead]
            half = gathered[part, :] + recv_terms[i - ahead]()[...]
            hidden = swish_of_half(half).astype(bf16)
            values = nt(edge_w()[...], hidden)
            index = index_row(recv_index, part) - place() * count
            sums.append(pick_rows(index, count))
            if waiting is not None:
                messages[:, waiting[0]] = norm_columns(waiting[1], gain).astype(bf16)
            waiting = (part, values)
    messages[:, waiting[0]] = norm_columns(waiting[1], gain).astype(bf16)
    nodes = nt(jnp.concatenate(sums, axis=1), messages[...]).astype(bf16)
    hidden = swish(nt(node_w()[...], nodes) + node_terms()[...]).astype(bf16)
    normed = norm_columns(nn(node_second_w()[...], hidden), column(gains, 3))
    values = (latent_columns()[...].astype(f32) + normed).astype(bf16)
    staged[...] = values
    copy = pltpu.make_async_copy(staged, state, semaphore)
    copy.start()
    sent = nn(send_w()[...], values).astype(bf16)
    send[...] = sent
    send_low[...] = sent[:, :reach]
    send_high[...] = sent[:, sent.shape[1] - reach :]
    copy.wait()


def local_kernel(index, *refs):
    *terms, send, out = refs
    for k in range(out.shape[0]):
        for part in blocks(out.shape[2]):
            picks = index()[k, :, part] - place() * send.shape[1]
            picks = pick_rows(picks, send.shape[1], 0.5)
            out[k, :, part] = terms[k]()[:, part] + nn(send[...], picks)


def decode_kernel(
    low,
    high,
    index,
    terms,
    edge_w,
    gains,
    gathered_w,
    out_terms,
    out_w,
    out_bias,
    prediction,
    staged,
    semaphores,
):
    halo = jnp.concatenate([low[...], high[...]], axis=1)
    gain = column(gains, 4)
    offset = out_bias[...].reshape(1, -1)
    offset = jnp.transpose(jnp.broadcast_to(offset, (8, offset.shape[1])))[:, :1]
    copies = []
    totals = {}
    last = terms.shape[0] - 1

    def first(spot):
        part, k = spot
        count = 2 * halo.shape[1]
        picks = outside(index[k, :, part] - place() * count, count, halo.shape[1] // 2)
        half = terms[k, :, part] + nn(halo, pick_rows(picks, halo.shape[1], 0.5))
        return nn(edge_w[...], swish_of_half(half).astype(bf16))

    def second(spot, values):
        part, k = spot
        message = norm_columns(values, gain).astype(bf16).astype(f32)
        totals[part.start] = message if k == 0 else totals[part.start] + message
        if k < last:
            return
        total = totals[part.start].astype(bf16)
        pre_act = out_terms[:, part] + nn(gathered_w[...], total)
        hidden = swish(pre_act).astype(bf16)
        staged[:, part] = nn(out_w[...], hidden) + offset
        copies.append(
            pltpu.make_async_copy(
                staged.at[:, part], prediction.at[:, part], semaphores.at[len(copies)]
            )
        )
        copies[-1].start()

    spots = [(part, k) for part in blocks(terms.shape[2]) for k in range(last + 1)]
    stagger(spots, first, second)
    for copy in copies:
        copy.wait()


def part_shape(shape, index):
    lead = tuple(part.size for part in index if isinstance(part, pl.Slice))
    return lead + shape[len(index) :]


def fetching(
    kernel,
    outs,
    fetched=(),
    resident=(),
    carried=(),
    scratch=(),
    in_place=(),
    limit=VMEM_LIMIT,
):
    pairs = [item if isinstance(item, tuple) else (item, ()) for item in fetched]
    n_in, n_res, n_out = len(pairs), len(resident), len(outs)
    extra = []
    for item in carried:
        if isinstance(item, int):
            extra.append(item)
        else:
            pairs.append(item if isinstance(item, tuple) else (item, ()))
            extra.append(len(pairs) - 1)
    arrays = [array for array, _ in pairs]
    shapes = [(part_shape(array.shape, index), array.dtype) for array, index in pairs]
    local = [i for i in range(len(pairs)) if i not in extra]

    def run(*refs):
        sources, refs = refs[: len(pairs)], refs[len(pairs) :]
        near, refs = refs[:n_res], refs[n_res:]
        results, refs = refs[:n_out], refs[n_out:]
        passed, refs = refs[: len(extra)], refs[len(extra) :]
        buffers = dict(zip(extra, passed))
        buffers.update(zip(local, refs[: len(local)]))
        refs = refs[len(local) :]
        copies = []
        if pairs:
            for i, (source, (_, index)) in enumerate(zip(sources, pairs)):
                source = source.at[index] if index else source
                copies.append(Fetch(source, buffers[i], refs[0].at[i]))
            refs = refs[1:]
        kernel(*copies[:n_in], *near, *results, *refs)
        for copy in copies:
            copy()

    near = pl.BlockSpec(memory_space=pltpu.VMEM)
    far = pl.BlockSpec(memory_space=pltpu.HBM)
    return pl.pallas_call(
        run,
        out_shape=tuple(outs) + tuple(pltpu.VMEM(*shapes[i]) for i in extra),
        in_specs=[far] * len(pairs) + [near] * n_res,
        out_specs=tuple(far if i in in_place else near for i in range(n_out))
        + (near,) * len(extra),
        scratch_shapes=[pltpu.VMEM(*shapes[i]) for i in local]
        + ([pltpu.SemaphoreType.DMA((len(pairs),))] if pairs else [])
        + list(scratch),
        compiler_params=pltpu.CompilerParams(vmem_limit_bytes=limit),
    )(
        *[pltpu.with_memory_space_constraint(value, pltpu.HBM) for value in arrays],
        *[pltpu.with_memory_space_constraint(value, pltpu.VMEM) for value in resident],
    )


def exchange(low_end, high_end):
    axes = ("space", "chan")
    count = lax.axis_size("space") * lax.axis_size("chan")
    up = [(i, (i + 1) % count) for i in range(count)]
    down = [(target, source) for source, target in up]
    low = lax.ppermute(high_end, axes, up)
    high = lax.ppermute(low_end, axes, down)
    return low, high


def body(
    grid_in,
    grid_embed_w,
    g2m_w,
    pair_w,
    second_w,
    first_b,
    norm_gain,
    geom_w,
    out_w,
    out_b,
    g2m_geom,
    mesh_geom,
    m2g_geom,
    g2m_send,
    g2m_recv,
    mesh_recv,
    mesh_slot,
    mesh_rows,
    m2g_send,
):
    width = grid_embed_w.shape[0]
    cells = grid_in.shape[1]
    reach = cells // 4
    low, high = exchange(grid_in[:, :reach], grid_in[:, cells - reach :])

    kept = pltpu.VMEM
    shape = pltpu.HBM
    embed_t = grid_embed_w.T
    geom_t = geom_w.transpose(0, 2, 1)
    edges = g2m_geom.shape[1]
    slots = mesh_rows.size
    (
        grid_latent,
        own_terms,
        sums,
        picks,
        embed_near,
        embed_second_near,
        g2m_near,
        bias_near,
        gain_near,
        send_near,
        edge_near,
        link_near,
    ) = fetching(
        embed_kernel,
        (
            kept((width, cells), bf16),
            kept((width, edges), f32),
            kept((M_DEV, edges), bf16),
            kept((slots, M_DEV), bf16),
        ),
        [
            grid_in,
            embed_t,
            first_b,
            (second_w, (0,)),
            norm_gain,
            g2m_w,
            g2m_send,
            g2m_geom,
            (geom_t, (0,)),
            g2m_recv,
            mesh_rows,
        ],
        carried=[1, 3, 5, 2, 4, 6, (second_w, (1,)), (pair_w, (0, 0))],
        scratch=[pltpu.VMEM((width, cells), bf16)],
    )

    grid_latent, latent, outgoing = fetching(
        encode_kernel,
        (
            shape((width, cells), bf16),
            shape((M_DEV, width), bf16),
            shape((slots, width), bf16),
        ),
        resident=[
            grid_latent,
            own_terms,
            sums,
            picks,
            low,
            high,
            embed_near,
            embed_second_near,
            g2m_near,
            bias_near,
            gain_near,
            send_near,
            edge_near,
            link_near,
        ],
        scratch=[
            pltpu.VMEM((width, edges), bf16),
            pltpu.VMEM((slots, width), bf16),
            pltpu.VMEM((M_DEV, width), bf16),
            pltpu.SemaphoreType.DMA((2 + slots // BLOCK,)),
        ],
        in_place=(0, 1, 2),
    )
    arrived = lax.all_to_all(
        outgoing.reshape(mesh_rows.shape + (width,)),
        ("space", "chan"),
        split_axis=0,
        concat_axis=0,
        tiled=True,
    ).reshape(-1, width)

    mesh_edges = mesh_geom.shape[1]
    mesh_reach = M_DEV // 4
    per_cell = m2g_send.shape[0] // cells
    cell_geom = m2g_geom.reshape(-1, cells, per_cell).transpose(2, 0, 1)
    cell_send = m2g_send.reshape(cells, per_cell).T[:, None, :]
    latent, cell_send = lax.optimization_barrier((latent, cell_send))
    recv_terms, node_terms, latent_columns, cell_terms, out_terms = fetching(
        window_kernel,
        (
            shape((mesh_edges, width), f32),
            shape((width, M_DEV), f32),
            shape((width, M_DEV), bf16),
            shape((per_cell, width, cells), f32),
            shape((width, cells), f32),
        ),
        [
            latent,
            mesh_geom,
            (pair_w, (0, 1)),
            first_b,
            (geom_t, (1,)),
            mesh_recv,
            (pair_w, (1, 0)),
            grid_latent,
            (pair_w, (2, 1)),
            (pair_w, (3, 0)),
            (geom_t, (2,)),
            cell_geom,
        ],
        limit=40 << 20,
    )

    state, send, send_low, send_high = fetching(
        mesh_kernel,
        (
            shape((width, M_DEV), bf16),
            kept((width, M_DEV), bf16),
            kept((width, mesh_reach), bf16),
            kept((width, mesh_reach), bf16),
        ),
        [(second_w, (2,))]
        + [(recv_terms, (part,)) for part in blocks(mesh_edges)]
        + [
            (pair_w, (1, 1)),
            node_terms,
            (second_w, (3,)),
            latent_columns,
            (pair_w, (2, 0)),
        ],
        resident=[mesh_slot, mesh_recv, norm_gain, arrived],
        scratch=[
            pltpu.VMEM((width, mesh_edges), bf16),
            pltpu.VMEM((mesh_edges, width), f32),
            pltpu.VMEM((width, M_DEV), bf16),
            pltpu.SemaphoreType.DMA(()),
        ],
        in_place=(0,),
        limit=32 << 20,
    )
    low, high = exchange(send_low, send_high)
    (
        cell_terms,
        send_near,
        decode_near,
        gain_near,
        gathered_near,
        out_terms,
        out_w_near,
        out_b_near,
    ) = fetching(
        local_kernel,
        (kept(cell_terms.shape, f32),),
        [cell_send] + [(cell_terms, (k,)) for k in range(per_cell)],
        resident=[send],
        carried=[
            0,
            (second_w, (4,)),
            norm_gain,
            (pair_w, (3, 1)),
            out_terms,
            out_w,
            out_b,
        ],
    )
    (prediction,) = fetching(
        decode_kernel,
        (shape((out_w.shape[0], cells), f32),),
        resident=[
            low,
            high,
            send_near,
            cell_terms,
            decode_near,
            gain_near,
            gathered_near,
            out_terms,
            out_w_near,
            out_b_near,
        ],
        scratch=[
            pltpu.VMEM((out_w.shape[0], cells), f32),
            pltpu.SemaphoreType.DMA((cells // BLOCK,)),
        ],
        in_place=(0,),
    )
    return (prediction, state)


def solution(mesh):
    split = ("space", "chan")
    return jax.shard_map(
        body,
        mesh=mesh,
        in_specs=(
            P(None, split),
            P(),
            P(),
            P(),
            P(),
            P(),
            P(),
            P(),
            P(),
            P(),
            P(None, split),
            P(None, split),
            P(None, split),
            P(split),
            P(split),
            P(split),
            P(split),
            P(split, None),
            P(split),
        ),
        out_specs=(P(None, split), P(None, split)),
        check_vma=False,
    )
```
